32 devices in a mesh: gx: 8 (over y, x, core), gy: 4 (over z).
Axes of the slice: x: 2, y: 2, z: 4, core: 2. Of those that a mesh axis runs over, the one named last changes fastest.
Arguments:
- state: float32 [4, 64, 2, 16, 512], P(None, None, None, 'gx', 'gy'), may hold values from -6 to 6
- register: float32 [4, 64, 2, 16, 512], P(None, None, None, 'gx', 'gy'), may hold values from -6 to 6
- cotangent: float32 [4, 64, 2, 16, 512], P(None, None, None, 'gx', 'gy'), may hold values from -6 to 6
- impedance: float32 [2048], P('gy'), may hold values from 0.2 to 5
- wall_patch: int32 [2, 16, 512], P(None, 'gx', 'gy'), may hold values from 0 to 2047
Outputs:
- next_state: float32 [4, 64, 2, 16, 512], P(None, None, None, 'gx', 'gy')
- next_register: float32 [4, 64, 2, 16, 512], P(None, None, None, 'gx', 'gy')
- state_gradient: float32 [4, 64, 2, 16, 512], P(None, None, None, 'gx', 'gy')
- impedance_gradient: float32 [2048], P('gy')
The draws below stay inside these ranges and needn't reach their ends.
All inputs are finite; a program needn't handle non-finite values.
Results may differ from the reference program's by a relative error of at most 0.00014.
Values sent between devices are 32-bit elements; how exact they have to be, the bound alone decides.
No kernel may reach another device: no remote copies, remote signals or barrier semaphores. Data moves between devices by JAX's collectives and lax.ppermute only.
A program may use at most 64 MiB of HBM per device.

```python
import math
import jax
import jax.numpy as jnp
import numpy as np
from jax import lax

FIELDS = 4
NODES = 64
NXE = 16
NYE = 512
NZE = 2
PATCHES = 2048


def place_ends(values, own_key, least, top_value):
    dims = values.shape
    place = [jax.random.randint(jax.random.fold_in(own_key, axis), (), 0, dims[axis]) for axis in range(len(dims))]
    values = values.at[tuple(place)].set(least)
    longest = dims.index(max(dims))
    place[longest] = (place[longest] + 1) % dims[longest]
    return values.at[tuple(place)].set(top_value)


def block_scale(stream_key, dims, split, smallest, high):
    factor_of, own = 1.0, jax.random.fold_in(stream_key, 6)
    for dim, blocks in split:
        draws = jnp.exp(jax.random.uniform(jax.random.fold_in(own, dim), (blocks,), jnp.float32, smallest / len(split), high / len(split)))
        factor_of = factor_of * jnp.repeat(draws, dims[dim] // blocks).reshape([-1 if axis == dim else 1 for axis in range(len(dims))])
    return factor_of


def normal_values(stream_key, extent, scale, limit, split=(), kind=jnp.bfloat16):
    gain = block_scale(stream_key, extent, split, -0.22, 0.18) if split else 1.0
    result = jax.random.normal(stream_key, extent, jnp.float32) * scale * gain
    return jnp.minimum(jnp.maximum(result, -limit), limit).astype(kind)


def setup_inputs(seed: int = 0) -> dict:
    seeds = jax.random.split(jax.random.key(seed), 6)
    return {
        "state": normal_values(seeds[0], (FIELDS, NODES, NZE, NXE, NYE), 1.0, 6.0, ((3, 8), (4, 4)), jnp.float32),
        "register": normal_values(seeds[1], (FIELDS, NODES, NZE, NXE, NYE), 1.0, 6.0, ((3, 8), (4, 4)), jnp.float32),
        "cotangent": normal_values(seeds[2], (FIELDS, NODES, NZE, NXE, NYE), 1.0, 6.0, ((3, 8), (4, 4)), jnp.float32),
        "impedance": jnp.clip(jnp.exp(math.log(5.0) - 3.218876 * jax.random.uniform(seeds[3], (PATCHES,), jnp.float32) ** block_scale(seeds[3], (PATCHES,), ((0, 4),), -0.2, 0.2)), 0.2, 5.0),
        "wall_patch": place_ends(jax.random.randint(seeds[4], (2, NXE, NYE), 0, PATCHES), jax.random.fold_in(seeds[4], 1), 0, PATCHES - 1).astype(jnp.int32),
    }


time_step = 0.02
section_a = -0.4178904745
section_b = 0.3792103129
lift_half = 6.0

def derivative_table():
    points = np.array([-1.0, -1.0 / math.sqrt(5.0), 1.0 / math.sqrt(5.0), 1.0])
    identity = np.array([[1.0 if row == col else 0.0 for col in range(4)] for row in range(4)])
    distance = points[:, None] - points[None, :] + identity
    barycentric = 1.0 / np.prod(distance, axis=1)
    matrix = barycentric[None, :] / (barycentric[:, None] * distance)
    matrix = matrix * (1.0 - identity)
    matrix = matrix - identity * matrix.sum(axis=1)[:, None]
    return jnp.asarray(2.0 * matrix, dtype=jnp.float32)

def along(matrix, values, spec):
    return jnp.einsum(spec, matrix, values, precision=lax.Precision.HIGHEST)

def face_jump(inside, outside, component, orient):
    jumps = outside - inside
    normal_jump = orient * jumps[component + 1]
    velocity = [lift_half * jumps[1], lift_half * jumps[2], lift_half * jumps[3]]
    velocity[component] = velocity[component] - lift_half * orient * jumps[0]
    return jnp.stack([lift_half * (jumps[0] - normal_jump)] + velocity)

def wall_term(inside, reflection, orient):
    pressure = inside[0]
    normal_speed = orient * inside[3]
    incoming = 0.5 * (reflection * (pressure + normal_speed) - (pressure - normal_speed))
    nothing = jnp.zeros_like(incoming)
    return jnp.stack([2.0 * lift_half * incoming, nothing, nothing, -2.0 * lift_half * orient * incoming])

def tendency_of(padded, reflection):
    matrix = derivative_table()
    inner = padded[..., 1:-1, 1:-1]
    pressure = inner[0]
    divergence = along(matrix, inner[1], 'ia,abczxy->ibczxy') + along(matrix, inner[2], 'jb,abczxy->ajczxy') + along(matrix, inner[3], 'kc,abczxy->abkzxy')
    tendency = jnp.stack([-divergence, -along(matrix, pressure, 'ia,abczxy->ibczxy'), -along(matrix, pressure, 'jb,abczxy->ajczxy'), -along(matrix, pressure, 'kc,abczxy->abkzxy')])
    tendency = tendency.at[:, 3].add(face_jump(inner[:, 3], padded[:, 0, :, :, :, 2:, 1:-1], 0, 1.0))
    tendency = tendency.at[:, 0].add(face_jump(inner[:, 0], padded[:, 3, :, :, :, :-2, 1:-1], 0, -1.0))
    tendency = tendency.at[:, :, 3].add(face_jump(inner[:, :, 3], padded[:, :, 0, :, :, 1:-1, 2:], 1, 1.0))
    tendency = tendency.at[:, :, 0].add(face_jump(inner[:, :, 0], padded[:, :, 3, :, :, 1:-1, :-2], 1, -1.0))
    upper = jnp.concatenate([face_jump(inner[:, :, :, 3, :-1], inner[:, :, :, 0, 1:], 2, 1.0), wall_term(inner[:, :, :, 3, -1:], reflection[1], 1.0)], axis=3)
    lower = jnp.concatenate([wall_term(inner[:, :, :, 0, :1], reflection[0], -1.0), face_jump(inner[:, :, :, 0, 1:], inner[:, :, :, 3, :-1], 2, -1.0)], axis=3)
    tendency = tendency.at[:, :, :, 3].add(upper)
    tendency = tendency.at[:, :, :, 0].add(lower)
    return tendency

def reference(state, register, cotangent, impedance, wall_patch):

    def advance(values, patch_values):
        cube = values.reshape(values.shape[:1] + (4, 4, 4) + values.shape[2:])
        padded = jnp.pad(cube, ((0, 0), (0, 0), (0, 0), (0, 0), (0, 0), (1, 1), (1, 1)), mode='wrap')
        chosen = patch_values[wall_patch]
        reflection = (chosen - 1.0) / (chosen + 1.0)
        return tendency_of(padded, reflection).reshape(values.shape)
    tendency, pullback = jax.vjp(advance, state, impedance)
    next_register = section_a * register + time_step * tendency
    next_state = state + section_b * next_register
    state_back, impedance_back = pullback(time_step * section_b * cotangent)
    return (next_state, next_register, cotangent + state_back, impedance_back)
```

```python
import functools
import math

import jax
import jax.numpy as jnp
import numpy as np
from jax import lax
from jax.experimental import pallas as pl
from jax.experimental.pallas import tpu as pltpu
from jax.sharding import PartitionSpec as P

time_step = 0.02
section_a = -0.4178904745
section_b = 0.3792103129
lift_half = 6.0

LANES = 128
HALO_LANES = 48
IMP_LANE = 48
SUM_LANE = 64


def derivative_table():
    points = np.array([-1.0, -1.0 / math.sqrt(5.0), 1.0 / math.sqrt(5.0), 1.0])
    identity = np.eye(4)
    distance = points[:, None] - points[None, :] + identity
    barycentric = 1.0 / np.prod(distance, axis=1)
    matrix = barycentric[None, :] / (barycentric[:, None] * distance)
    matrix = matrix * (1.0 - identity)
    matrix = matrix - identity * matrix.sum(axis=1)[:, None]
    return 2.0 * matrix


def row_of(field, a, b, half):
    return field * 256 + a * 64 + b * 16 + half * 8


def load(ref, field, a, b, half):
    return ref[pl.ds(row_of(field, a, b, half), 8), :]


def sub_roll(value, shift):
    return pltpu.roll(value, shift % 8, 0)


def lane_roll(value, shift):
    shift = shift % LANES
    return value if shift == 0 else pltpu.roll(value, shift, 1)


def rows_iota():
    return lax.broadcasted_iota(jnp.int32, (8, LANES), 0)


def lanes_iota():
    return lax.broadcasted_iota(jnp.int32, (8, LANES), 1)


def x_trace(ref, sigma, a, b, half):
    flip = sigma if a == 3 else -sigma
    press, normal = load(ref, 0, a, b, half), load(ref, 1, a, b, half)
    mixed = press + normal if flip > 0 else press - normal
    return [mixed, load(ref, 2, a, b, half), load(ref, 3, a, b, half)]


def y_trace(ref, sigma, a, b, half):
    flip = sigma if b == 3 else -sigma
    press, normal = load(ref, 0, a, b, half), load(ref, 2, a, b, half)
    mixed = press + normal if flip > 0 else press - normal
    return [mixed, load(ref, 1, a, b, half), load(ref, 3, a, b, half)]


def pack_kernel(gx, gy, st, ct, imp, wp, first, second, chunks):
    me_x, me_y = lax.axis_index("gx"), lax.axis_index("gy")
    rows, lanes = rows_iota(), lanes_iota()
    even_row = (rows & 1) == 0
    even_me = (me_x & 1) == 0
    for number, (ref, sigma) in enumerate(((st, 1), (ct, -1))):
        for b in range(4):
            high = [x_trace(ref, sigma, 3, b, half) for half in range(2)]
            low = [x_trace(ref, sigma, 0, b, half) for half in range(2)]
            for part in range(3):
                to_right = jnp.where(even_row, sub_roll(high[0][part], -1), high[1][part])
                to_left = jnp.where(even_row, low[1][part], sub_roll(low[0][part], 1))
                at = pl.ds(((number * 3 + part) * 4 + b) * 8, 8)
                first[at, :] = jnp.where(even_me, to_right, to_left)
                second[at, :] = jnp.where(even_me, to_left, to_right)
    up = jnp.zeros((8, LANES), jnp.float32)
    down = jnp.zeros((8, LANES), jnp.float32)
    for number, (ref, sigma) in enumerate(((st, 1), (ct, -1))):
        for a in range(4):
            for half in range(2):
                high = y_trace(ref, sigma, a, 3, half)
                low = y_trace(ref, sigma, a, 0, half)
                for part in range(3):
                    k = (number * 3 + part) * 8 + a * 2 + half
                    up = jnp.where(lanes == k, lane_roll(high[part], k - 127), up)
                    down = jnp.where(lanes == k, lane_roll(low[part], k), down)
    floor = jnp.zeros((8, LANES), jnp.float32)
    ceil = jnp.zeros((8, LANES), jnp.float32)
    for a in range(4):
        for b in range(4):
            floor += (load(st, 0, a, b, 0) - load(st, 3, a, b, 0)) * (
                load(ct, 0, a, b, 0) + load(ct, 3, a, b, 0)
            )
            ceil += (load(st, 0, a, b, 1) + load(st, 3, a, b, 1)) * (
                load(ct, 0, a, b, 1) - load(ct, 3, a, b, 1)
            )
    values = jnp.concatenate([floor[0:1], floor[1:2], ceil[6:7], ceil[7:8]], axis=1)
    patch = jnp.concatenate([wp[r : r + 1, :] for r in range(4)], axis=1)
    groups = 4 * gy
    count = 4 * LANES
    high_of = lax.shift_right_logical(patch, 7)
    low_of = patch & (LANES - 1)
    chosen = lax.broadcasted_iota(jnp.int32, (groups, count), 0) == high_of
    spread = jnp.where(chosen, jnp.broadcast_to(values, (groups, count)), 0.0)
    top = spread.astype(jnp.bfloat16)
    rest = spread - top.astype(jnp.float32)
    middle = rest.astype(jnp.bfloat16)
    last = (rest - middle.astype(jnp.float32)).astype(jnp.bfloat16)
    pieces = jnp.concatenate([top, middle, last], axis=0)
    hot = lax.broadcasted_iota(jnp.int32, (LANES, count), 0) == low_of
    hot = jnp.where(hot, 1.0, 0.0).astype(jnp.bfloat16)
    sums = lax.dot_general(
        pieces, hot, (((1,), (1,)), ((), ())), preferred_element_type=jnp.float32
    )
    sums = sums[:groups] + sums[groups : 2 * groups] + sums[2 * groups :]
    width = LANES // gx
    shard = jnp.concatenate([imp[...], imp[...]], axis=0)
    placed = pltpu.roll(shard, (IMP_LANE - me_x * width + LANES) % LANES, 1)
    odd_me_y = me_y & 1
    imp_here = (
        (lanes >= IMP_LANE)
        & (lanes < IMP_LANE + width)
        & (lax.shift_right_logical(rows, 2) == odd_me_y)
    )
    common = jnp.where(imp_here, placed, 0.0)
    upper_lanes = lanes >= SUM_LANE
    tiles = []
    for target in range(gy):
        part = sums[target * 4 : target * 4 + 4]
        both = jnp.concatenate([pltpu.roll(part, SUM_LANE, 1), part], axis=0)
        tiles.append(jnp.where(upper_lanes, both, common))
    for x in range(gx):
        for target in range(gy):
            chunks[x * gy + target] = tiles[target]
    halo_lanes = lanes < HALO_LANES
    next_y = me_x * gy + lax.rem(me_y + 1, gy)
    prev_y = me_x * gy + lax.rem(me_y + gy - 1, gy)
    chunks[next_y] = jnp.where(halo_lanes, up, chunks[next_y])
    chunks[prev_y] = jnp.where(halo_lanes, down, chunks[prev_y])


def one_section(ref, sigma, matrix, scale, x_low, x_high, y_low, y_high, reflect, emit):
    rows = rows_iota()
    lower = rows < 4
    m = matrix * scale

    def pair(first, second):
        return jnp.where(lower, jnp.float32(first), jnp.float32(second))

    to_low = [pair(m[0, 1], m[1, 0]), pair(m[0, 2], m[1, 3]), pair(m[0, 3], m[1, 2])]
    to_high = [pair(m[2, 0], m[3, 1]), pair(m[2, 1], m[3, 0]), pair(m[2, 3], m[3, 2])]
    lift = jnp.float32(lift_half * scale)
    six = [
        jnp.where((rows >= 2) & (rows < 4), lift, 0.0),
        jnp.where((rows >= 4) & (rows < 6), lift, 0.0),
    ]
    wall = [
        jnp.where(rows < 2, reflect * lift, 0.0),
        jnp.where(rows >= 6, reflect * lift, 0.0),
    ]
    z_face = [lower, rows >= 4]
    lanes = lanes_iota()
    even_row = (rows & 1) == 0

    def own(count, half, inner_only):
        face = (six[half] > 0.0) if inner_only else z_face[half]
        return jnp.where(face, -lift * (count + 1), -lift * count)

    diagonal = {
        (count, half, inner): own(count, half, inner)
        for count in range(3)
        for half in range(2)
        for inner in (False, True)
    }

    def weighted(field, fixed, index, axis):
        total = None
        for other in range(4):
            if other == index:
                continue
            a, b, half = fixed
            if axis == 0:
                a = other
            else:
                b = other
            term = jnp.float32(m[index, other]) * load(ref, field, a, b, half)
            total = term if total is None else total + term
        return total

    for a in range(4):
        for b in range(4):
            press = [load(ref, 0, a, b, h) for h in range(2)]
            vel = [[load(ref, 1 + i, a, b, h) for h in range(2)] for i in range(3)]

            def c_weighted(values, half):
                rolled = [sub_roll(v, 4) for v in values]
                if half == 0:
                    return (
                        to_low[0] * rolled[0] + to_low[1] * values[1] + to_low[2] * rolled[1]
                    )
                return (
                    to_high[0] * values[0] + to_high[1] * rolled[0] + to_high[2] * rolled[1]
                )

            sign = jnp.float32(sigma)
            e0 = press[0] - vel[2][0] if sigma > 0 else press[0] + vel[2][0]
            e1 = press[1] + vel[2][1] if sigma > 0 else press[1] - vel[2][1]
            z_terms = [
                six[0] * sub_roll(e1, -2) + wall[0] * e0,
                six[1] * sub_roll(e0, 2) + wall[1] * e1,
            ]
            count = (1 if a in (0, 3) else 0) + (1 if b in (0, 3) else 0)
            for half in range(2):
                fixed = (a, b, half)
                out_p = (
                    weighted(1, fixed, a, 0)
                    + weighted(2, fixed, b, 1)
                    + c_weighted(vel[2], half)
                )
                out_1 = weighted(0, fixed, a, 0)
                out_2 = weighted(0, fixed, b, 1)
                out_3 = c_weighted(press, half)
                out_p = out_p + diagonal[count, half, False] * press[half] + z_terms[half]
                out_1 = out_1 + diagonal[count, half, True] * vel[0][half]
                out_2 = out_2 + diagonal[count, half, True] * vel[1][half]
                out_3 = out_3 + diagonal[count, half, False] * vel[2][half]
                plus = (sigma > 0) == (half == 0)
                out_3 = out_3 + z_terms[half] if plus else out_3 - z_terms[half]
                turn = -2 if half == 0 else 2
                out_1 = out_1 + six[half] * sub_roll(vel[0][1 - half], turn)
                out_2 = out_2 + six[half] * sub_roll(vel[1][1 - half], turn)
                if a in (0, 3):
                    theirs = x_trace(ref, sigma, 3 - a, b, half)
                    if a == 0:
                        near = [
                            jnp.where(even_row, x_low(part, b, half), sub_roll(t, 1))
                            for part, t in enumerate(theirs)
                        ]
                    else:
                        near = [
                            jnp.where(even_row, sub_roll(t, -1), x_high(part, b, half))
                            for part, t in enumerate(theirs)
                        ]
                    near = [lift * n for n in near]
                    out_p = out_p + near[0]
                    plus = (sigma > 0) == (a == 0)
                    out_1 = out_1 + near[0] if plus else out_1 - near[0]
                    out_2 = out_2 + near[1]
                    out_3 = out_3 + near[2]
                if b in (0, 3):
                    theirs = y_trace(ref, sigma, a, 3 - b, half)
                    if b == 0:
                        near = [
                            jnp.where(lanes == 0, y_low(part, a, half), lane_roll(t, 1))
                            for part, t in enumerate(theirs)
                        ]
                    else:
                        near = [
                            jnp.where(lanes == 127, y_high(part, a, half), lane_roll(t, -1))
                            for part, t in enumerate(theirs)
                        ]
                    near = [lift * n for n in near]
                    out_p = out_p + near[0]
                    plus = (sigma > 0) == (b == 0)
                    out_2 = out_2 + near[0] if plus else out_2 - near[0]
                    out_1 = out_1 + near[1]
                    out_3 = out_3 + near[2]
                emit(a, b, half, [out_p, out_1, out_2, out_3])


def section_kernel(
    gx, gy, st, rg, ct, imp, wp, first, second, chunks, new_st, new_rg, grad, imp_grad, table
):
    me_x, me_y = lax.axis_index("gx"), lax.axis_index("gy")
    rows, lanes = rows_iota(), lanes_iota()
    even_me = (me_x & 1) == 0
    width = LANES // gx
    total = None
    blocks = []
    for group in range(gy // 2):
        block = jnp.zeros((8, LANES), jnp.float32)
        for x in range(gx):
            pair = chunks[x * gy + 2 * group] + chunks[x * gy + 2 * group + 1]
            total = pair if total is None else total + pair
            moved = lane_roll(pair, x * width - IMP_LANE)
            here = (lanes >= x * width) & (lanes < (x + 1) * width)
            block = jnp.where(here, moved, block)
        table[group * 8 : group * 8 + 8, :] = (block - 1.0) / (block + 1.0)
    patch_sum = jnp.where(
        lanes < SUM_LANE, pltpu.roll(total, SUM_LANE, 1), sub_roll(total, 4)
    )[:4]
    above = imp[...] + 1.0
    factor = time_step * section_b * lift_half * 2.0
    imp_grad[...] = patch_sum * jnp.float32(factor) / (above * above)
    patch = jnp.concatenate([wp[...], wp[...]], axis=0)
    low_of = patch & (LANES - 1)
    high_of = lax.shift_right_logical(patch, 7)
    reflect = jnp.zeros((8, LANES), jnp.float32)
    for high in range(4 * gy):
        line = jnp.broadcast_to(table[high : high + 1, :], (8, LANES))
        found = jnp.take_along_axis(line, low_of, axis=1)
        reflect = jnp.where(high_of == high, found, reflect)

    below = chunks[me_x * gy + lax.rem(me_y + gy - 1, gy)]
    ahead = chunks[me_x * gy + lax.rem(me_y + 1, gy)]

    def halos(number):
        def at(part, b):
            return pl.ds(((number * 3 + part) * 4 + b) * 8, 8)

        def x_low(part, b, half):
            got = jnp.where(even_me, second[at(part, b), :], first[at(part, b), :])
            return got if half == 0 else sub_roll(got, -1)

        def x_high(part, b, half):
            got = jnp.where(even_me, first[at(part, b), :], second[at(part, b), :])
            return got if half == 0 else sub_roll(got, 1)

        def lane(part, a, half):
            return (number * 3 + part) * 8 + a * 2 + half

        def y_low(part, a, half):
            return lane_roll(below, -lane(part, a, half))

        def y_high(part, a, half):
            return lane_roll(ahead, 127 - lane(part, a, half))

        return x_low, x_high, y_low, y_high

    matrix = derivative_table()
    matrix = matrix * (1.0 - np.eye(4))

    def emit_state(a, b, half, outs):
        for field in range(4):
            at = pl.ds(row_of(field, a, b, half), 8)
            following = jnp.float32(section_a) * rg[at, :] + outs[field]
            new_rg[at, :] = following
            new_st[at, :] = st[at, :] + jnp.float32(section_b) * following

    def emit_grad(a, b, half, outs):
        for field in range(4):
            at = pl.ds(row_of(field, a, b, half), 8)
            grad[at, :] = ct[at, :] + outs[field]

    one_section(st, 1, -matrix, time_step, *halos(0), reflect, emit_state)
    one_section(ct, -1, -matrix.T, time_step * section_b, *halos(1), reflect, emit_grad)


def per_device(state, register, cotangent, impedance, wall_patch):
    gx, gy = lax.axis_size("gx"), lax.axis_size("gy")
    flat = (1024, LANES)
    st, rg, ct = (v.reshape(flat) for v in (state, register, cotangent))
    imp = impedance.reshape(4, LANES)
    wp = wall_patch.reshape(4, LANES)
    f32 = jnp.float32
    first, second, chunks = pl.pallas_call(
        functools.partial(pack_kernel, gx, gy),
        out_shape=(
            jax.ShapeDtypeStruct((192, LANES), f32),
            jax.ShapeDtypeStruct((192, LANES), f32),
            jax.ShapeDtypeStruct((gx * gy, 8, LANES), f32),
        ),
        name="pack",
    )(st, ct, imp, wp)
    near = [(i, i ^ 1) for i in range(gx)]
    far = [(i, (i + 1) % gx if i % 2 else (i - 1) % gx) for i in range(gx)]
    first = lax.ppermute(first, "gx", near)
    second = lax.ppermute(second, "gx", far)
    chunks = lax.all_to_all(chunks, ("gx", "gy"), 0, 0)
    new_st, new_rg, grad, imp_grad = pl.pallas_call(
        functools.partial(section_kernel, gx, gy),
        out_shape=(
            jax.ShapeDtypeStruct(flat, f32),
            jax.ShapeDtypeStruct(flat, f32),
            jax.ShapeDtypeStruct(flat, f32),
            jax.ShapeDtypeStruct((4, LANES), f32),
        ),
        scratch_shapes=[pltpu.VMEM((4 * gy, LANES), f32)],
        compiler_params=pltpu.CompilerParams(vmem_limit_bytes=24 * 2**20),
        name="section",
    )(st, rg, ct, imp, wp, first, second, chunks)
    return (
        new_st.reshape(state.shape),
        new_rg.reshape(state.shape),
        grad.reshape(state.shape),
        imp_grad.reshape(impedance.shape),
    )


def solution(mesh):
    fields = P(None, None, None, "gx", "gy")
    return jax.shard_map(
        per_device,
        mesh=mesh,
        in_specs=(fields, fields, fields, P("gy"), P(None, "gx", "gy")),
        out_specs=(fields, fields, fields, P("gy")),
        check_vma=False,
    )
```

```python
import functools
import math

import jax
import jax.numpy as jnp
import numpy as np
from jax import lax
from jax.experimental import pallas as pl
from jax.experimental.pallas import tpu as pltpu
from jax.sharding import PartitionSpec as P

time_step = 0.02
section_a = -0.4178904745
section_b = 0.3792103129
lift_half = 6.0

LANES = 128
HALO_LANES = 48
IMP_LANE = 48
SUM_LANE = 64


def derivative_table():
    points = np.array([-1.0, -1.0 / math.sqrt(5.0), 1.0 / math.sqrt(5.0), 1.0])
    identity = np.eye(4)
    distance = points[:, None] - points[None, :] + identity
    barycentric = 1.0 / np.prod(distance, axis=1)
    matrix = barycentric[None, :] / (barycentric[:, None] * distance)
    matrix = matrix * (1.0 - identity)
    matrix = matrix - identity * matrix.sum(axis=1)[:, None]
    return 2.0 * matrix


def rows_at(b, half):
    return pl.ds(b * 16 + half * 8, 8)


def load(ref, field, a, b, half):
    return ref[field, a, rows_at(b, half), :]


INTERIOR_FLOPS = 30000000000


def sub_roll(value, shift):
    return pltpu.roll(value, shift % 8, 0)


def lane_roll(value, shift):
    shift = shift % LANES
    return value if shift == 0 else pltpu.roll(value, shift, 1)


def rows_iota():
    return lax.broadcasted_iota(jnp.int32, (8, LANES), 0)


def lanes_iota():
    return lax.broadcasted_iota(jnp.int32, (8, LANES), 1)


def x_trace(ref, sigma, a, b, half):
    flip = sigma if a == 3 else -sigma
    press, normal = load(ref, 0, a, b, half), load(ref, 1, a, b, half)
    mixed = press + normal if flip > 0 else press - normal
    return [mixed, load(ref, 2, a, b, half), load(ref, 3, a, b, half)]


def y_trace(ref, sigma, a, b, half):
    flip = sigma if b == 3 else -sigma
    press, normal = load(ref, 0, a, b, half), load(ref, 2, a, b, half)
    mixed = press + normal if flip > 0 else press - normal
    return [mixed, load(ref, 1, a, b, half), load(ref, 3, a, b, half)]


def pack_kernel(
    gx, gy, st_in, ct_in, imp_in, wp_in, st, ct, imp, wp, first, second, chunks, sems, small, one_hot
):
    me_x, me_y = lax.axis_index("gx"), lax.axis_index("gy")
    rows, lanes = rows_iota(), lanes_iota()
    even_row = (rows & 1) == 0
    even_me = (me_x & 1) == 0
    loads = {}
    for number, (source, target) in enumerate(((imp_in, imp), (wp_in, wp))):
        loads[number, 4] = pltpu.make_async_copy(source, target, small.at[number])
    loads[1, 4].start()
    for a in (0, 3, 1, 2):
        for number, (source, target) in enumerate(((st_in, st), (ct_in, ct))):
            loads[number, a] = pltpu.make_async_copy(
                source.at[:, a], target.at[:, a], sems.at[number, a]
            )
            loads[number, a].start()
    loads[0, 4].start()
    up = jnp.zeros((8, LANES), jnp.float32)
    down = jnp.zeros((8, LANES), jnp.float32)
    floor = jnp.zeros((8, LANES), jnp.float32)
    ceil = jnp.zeros((8, LANES), jnp.float32)

    def columns_and_walls(a, up, down, floor, ceil):
        for number, (ref, sigma) in enumerate(((st, 1), (ct, -1))):
            for half in range(2):
                high = y_trace(ref, sigma, a, 3, half)
                low = y_trace(ref, sigma, a, 0, half)
                for part in range(3):
                    k = (number * 3 + part) * 8 + a * 2 + half
                    up = jnp.where(lanes == k, lane_roll(high[part], k - 127), up)
                    down = jnp.where(lanes == k, lane_roll(low[part], k), down)
        for b in range(4):
            floor += (load(st, 0, a, b, 0) - load(st, 3, a, b, 0)) * (
                load(ct, 0, a, b, 0) + load(ct, 3, a, b, 0)
            )
            ceil += (load(st, 0, a, b, 1) + load(st, 3, a, b, 1)) * (
                load(ct, 0, a, b, 1) - load(ct, 3, a, b, 1)
            )
        return up, down, floor, ceil

    loads[1, 4].wait()
    groups = 4 * gy
    count = 4 * LANES
    patch = jnp.concatenate([wp[r : r + 1, :] for r in range(4)], axis=1)
    high_of = lax.shift_right_logical(patch, 7)
    low_of = patch & (LANES - 1)
    hot = lax.broadcasted_iota(jnp.int32, (LANES, count), 0) == low_of
    one_hot[...] = jnp.where(hot, 1.0, 0.0).astype(jnp.bfloat16)
    loads[0, 0].wait()
    loads[1, 0].wait()
    up, down, floor, ceil = columns_and_walls(0, up, down, floor, ceil)
    loads[0, 3].wait()
    loads[1, 3].wait()
    up, down, floor, ceil = columns_and_walls(3, up, down, floor, ceil)
    for number, (ref, sigma) in enumerate(((st, 1), (ct, -1))):
        for b in range(4):
            high = [x_trace(ref, sigma, 3, b, half) for half in range(2)]
            low = [x_trace(ref, sigma, 0, b, half) for half in range(2)]
            for part in range(3):
                to_right = jnp.where(even_row, sub_roll(high[0][part], -1), high[1][part])
                to_left = jnp.where(even_row, low[1][part], sub_roll(low[0][part], 1))
                at = pl.ds(((number * 3 + part) * 4 + b) * 8, 8)
                first[at, :] = jnp.where(even_me, to_right, to_left)
                second[at, :] = jnp.where(even_me, to_left, to_right)
    for a in (1, 2):
        loads[0, a].wait()
        loads[1, a].wait()
        up, down, floor, ceil = columns_and_walls(a, up, down, floor, ceil)
    loads[0, 4].wait()
    values = jnp.concatenate([floor[0:1], floor[1:2], ceil[6:7], ceil[7:8]], axis=1)
    chosen = lax.broadcasted_iota(jnp.int32, (groups, count), 0) == high_of
    spread = jnp.where(chosen, jnp.broadcast_to(values, (groups, count)), 0.0)
    top = spread.astype(jnp.bfloat16)
    rest = spread - top.astype(jnp.float32)
    middle = rest.astype(jnp.bfloat16)
    last = (rest - middle.astype(jnp.float32)).astype(jnp.bfloat16)
    pieces = jnp.concatenate([top, middle, last], axis=0)
    sums = lax.dot_general(
        pieces, one_hot[...], (((1,), (1,)), ((), ())), preferred_element_type=jnp.float32
    )
    sums = sums[:groups] + sums[groups : 2 * groups] + sums[2 * groups :]
    width = LANES // gx
    shard = jnp.concatenate([imp[...], imp[...]], axis=0)
    placed = pltpu.roll(shard, (IMP_LANE - me_x * width + LANES) % LANES, 1)
    odd_me_y = me_y & 1
    imp_here = (
        (lanes >= IMP_LANE)
        & (lanes < IMP_LANE + width)
        & (lax.shift_right_logical(rows, 2) == odd_me_y)
    )
    common = jnp.where(imp_here, placed, 0.0)
    upper_lanes = lanes >= SUM_LANE
    tiles = []
    for target in range(gy):
        part = sums[target * 4 : target * 4 + 4]
        both = jnp.concatenate([pltpu.roll(part, SUM_LANE, 1), part], axis=0)
        tiles.append(jnp.where(upper_lanes, both, common))
    for x in range(gx):
        for target in range(gy):
            chunks[x * gy + target] = tiles[target]
    halo_lanes = lanes < HALO_LANES
    next_y = me_x * gy + lax.rem(me_y + 1, gy)
    prev_y = me_x * gy + lax.rem(me_y + gy - 1, gy)
    chunks[next_y] = jnp.where(halo_lanes, up, chunks[next_y])
    chunks[prev_y] = jnp.where(halo_lanes, down, chunks[prev_y])


def interior(ref, sigma, matrix, scale, x_low, x_high, emit):
    rows = rows_iota()
    lower = rows < 4
    m = matrix * scale

    def pair(first, second):
        return jnp.where(lower, jnp.float32(first), jnp.float32(second))

    to_low = [pair(m[0, 1], m[1, 0]), pair(m[0, 2], m[1, 3]), pair(m[0, 3], m[1, 2])]
    to_high = [pair(m[2, 0], m[3, 1]), pair(m[2, 1], m[3, 0]), pair(m[2, 3], m[3, 2])]
    lift = jnp.float32(lift_half * scale)
    six = [
        jnp.where((rows >= 2) & (rows < 4), lift, 0.0),
        jnp.where((rows >= 4) & (rows < 6), lift, 0.0),
    ]
    z_face = [lower, rows >= 4]
    lanes = lanes_iota()
    even_row = (rows & 1) == 0

    def own(count, half, inner_only):
        face = (six[half] > 0.0) if inner_only else z_face[half]
        return jnp.where(face, -lift * (count + 1), -lift * count)

    diagonal = {
        (count, half, inner): own(count, half, inner)
        for count in range(3)
        for half in range(2)
        for inner in (False, True)
    }

    def weighted(field, fixed, index, axis):
        total = None
        for other in range(4):
            if other == index:
                continue
            a, b, half = fixed
            if axis == 0:
                a = other
            else:
                b = other
            term = jnp.float32(m[index, other]) * load(ref, field, a, b, half)
            total = term if total is None else total + term
        return total

    def c_weighted(values, rolled, half):
        if half == 0:
            return to_low[0] * rolled[0] + to_low[1] * values[1] + to_low[2] * rolled[1]
        return to_high[0] * values[0] + to_high[1] * rolled[0] + to_high[2] * rolled[1]

    for a in range(4):
        for b in range(4):
            press = [load(ref, 0, a, b, h) for h in range(2)]
            vel = [[load(ref, 1 + i, a, b, h) for h in range(2)] for i in range(3)]
            press_rolled = [sub_roll(v, 4) for v in press]
            up_rolled = [sub_roll(v, 4) for v in vel[2]]
            e0, e1 = wall_traces(press, vel[2], sigma)
            z_terms = [six[0] * sub_roll(e1, -2), six[1] * sub_roll(e0, 2)]
            count = (1 if a in (0, 3) else 0) + (1 if b in (0, 3) else 0)
            for half in range(2):
                fixed = (a, b, half)
                out_p = (
                    weighted(1, fixed, a, 0)
                    + weighted(2, fixed, b, 1)
                    + c_weighted(vel[2], up_rolled, half)
                )
                out_1 = weighted(0, fixed, a, 0)
                out_2 = weighted(0, fixed, b, 1)
                out_3 = c_weighted(press, press_rolled, half)
                out_p = out_p + diagonal[count, half, False] * press[half] + z_terms[half]
                out_1 = out_1 + diagonal[count, half, True] * vel[0][half]
                out_2 = out_2 + diagonal[count, half, True] * vel[1][half]
                out_3 = out_3 + diagonal[count, half, False] * vel[2][half]
                plus = (sigma > 0) == (half == 0)
                out_3 = out_3 + z_terms[half] if plus else out_3 - z_terms[half]
                turn = -2 if half == 0 else 2
                out_1 = out_1 + six[half] * sub_roll(vel[0][1 - half], turn)
                out_2 = out_2 + six[half] * sub_roll(vel[1][1 - half], turn)
                if a in (0, 3):
                    theirs = x_trace(ref, sigma, 3 - a, b, half)
                    if a == 0:
                        near = [
                            jnp.where(even_row, x_low(part, b, half), sub_roll(t, 1))
                            for part, t in enumerate(theirs)
                        ]
                    else:
                        near = [
                            jnp.where(even_row, sub_roll(t, -1), x_high(part, b, half))
                            for part, t in enumerate(theirs)
                        ]
                    near = [lift * n for n in near]
                    out_p = out_p + near[0]
                    plus = (sigma > 0) == (a == 0)
                    out_1 = out_1 + near[0] if plus else out_1 - near[0]
                    out_2 = out_2 + near[1]
                    out_3 = out_3 + near[2]
                if b in (0, 3):
                    theirs = y_trace(ref, sigma, a, 3 - b, half)
                    if b == 0:
                        weight = jnp.where(lanes == 0, 0.0, lift)
                        near = [weight * lane_roll(t, 1) for t in theirs]
                    else:
                        weight = jnp.where(lanes == 127, 0.0, lift)
                        near = [weight * lane_roll(t, -1) for t in theirs]
                    out_p = out_p + near[0]
                    plus = (sigma > 0) == (b == 0)
                    out_2 = out_2 + near[0] if plus else out_2 - near[0]
                    out_1 = out_1 + near[1]
                    out_3 = out_3 + near[2]
                emit(a, b, half, (out_p, out_1, out_2, out_3))


def wall_traces(press, vertical, sigma):
    if sigma > 0:
        return press[0] - vertical[0], press[1] + vertical[1]
    return press[0] + vertical[0], press[1] - vertical[1]


def interior_kernel(
    st, ct, first, second, rg_in, new_st, new_rg, grad, st_out, rg_out, grad_out, rg, sems
):
    me_x = lax.axis_index("gx")
    load_rg = pltpu.make_async_copy(rg_in, rg, sems.at[3])
    load_rg.start()
    even_me = (me_x & 1) == 0

    def halos(number):
        def at(part, b):
            return pl.ds(((number * 3 + part) * 4 + b) * 8, 8)

        def x_low(part, b, half):
            got = jnp.where(even_me, second[at(part, b), :], first[at(part, b), :])
            return got if half == 0 else sub_roll(got, -1)

        def x_high(part, b, half):
            got = jnp.where(even_me, first[at(part, b), :], second[at(part, b), :])
            return got if half == 0 else sub_roll(got, 1)

        return x_low, x_high

    matrix = derivative_table()
    matrix = matrix * (1.0 - np.eye(4))

    def store(source, target, kind):
        inner = (pl.ds(1, 2), slice(None), pl.ds(16, 32))
        copy = pltpu.make_async_copy(source.at[inner], target.at[inner], sems.at[kind])
        copy.start()
        return copy

    def emit_grad(a, b, half, outs):
        at = rows_at(b, half)
        for field in range(4):
            grad[field, a, at, :] = ct[field, a, at, :] + outs[field]

    def emit_state(a, b, half, outs):
        at = rows_at(b, half)
        for field in range(4):
            following = jnp.float32(section_a) * rg[field, a, at, :] + outs[field]
            new_rg[field, a, at, :] = following
            new_st[field, a, at, :] = st[field, a, at, :] + jnp.float32(section_b) * following

    interior(ct, -1, -matrix.T, time_step * section_b, *halos(1), emit_grad)
    stores = [store(grad, grad_out, 2)]
    load_rg.wait()
    interior(st, 1, -matrix, time_step, *halos(0), emit_state)
    stores += [store(new_st, st_out, 0), store(new_rg, rg_out, 1)]
    for copy in stores:
        copy.wait()


def finish_kernel(
    gx,
    gy,
    st,
    ct,
    imp,
    wp,
    new_st,
    new_rg,
    grad,
    chunks,
    st_prior,
    rg_prior,
    grad_prior,
    st_out,
    rg_out,
    grad_out,
    imp_out,
    table,
    imp_grad,
    full_st,
    full_rg,
    full_grad,
    sems,
    last_sem,
):
    del st_prior, rg_prior, grad_prior
    me_x, me_y = lax.axis_index("gx"), lax.axis_index("gy")
    rows, lanes = rows_iota(), lanes_iota()
    stores = []

    def store(source, target, at, kind, piece):
        copy = pltpu.make_async_copy(source.at[at], target.at[at], sems.at[kind, piece])
        copy.start()
        stores.append(copy)

    def store_lines(source, target, b, kind):
        every = slice(None)
        if b in (0, 3):
            store(source, target, (every, every, pl.ds(b * 16, 16)), kind, b)
        if b == 2:
            for piece, field in ((1, 0), (2, 3)):
                at = (pl.ds(field, 1), every, pl.ds(16, 32))
                store(source, target, at, kind, piece)

    width = LANES // gx
    total = None
    for group in range(gy // 2):
        block = jnp.zeros((8, LANES), jnp.float32)
        for x in range(gx):
            pair = chunks[x * gy + 2 * group] + chunks[x * gy + 2 * group + 1]
            total = pair if total is None else total + pair
            moved = lane_roll(pair, x * width - IMP_LANE)
            here = (lanes >= x * width) & (lanes < (x + 1) * width)
            block = jnp.where(here, moved, block)
        table[group * 8 : group * 8 + 8, :] = (block - 1.0) / (block + 1.0)
    patch_sum = jnp.where(
        lanes < SUM_LANE, pltpu.roll(total, SUM_LANE, 1), sub_roll(total, 4)
    )[:4]
    above = imp[...] + 1.0
    factor = time_step * section_b * lift_half * 2.0
    imp_grad[...] = patch_sum * jnp.float32(factor) / (above * above)
    send_sum = pltpu.make_async_copy(imp_grad, imp_out, last_sem.at[0])
    send_sum.start()
    patch = jnp.concatenate([wp[...], wp[...]], axis=0)
    low_of = patch & (LANES - 1)
    high_of = lax.shift_right_logical(patch, 7)
    reflect = jnp.zeros((8, LANES), jnp.float32)
    for high in range(4 * gy):
        line = jnp.broadcast_to(table[high : high + 1, :], (8, LANES))
        found = jnp.take_along_axis(line, low_of, axis=1)
        reflect = jnp.where(high_of == high, found, reflect)

    below = chunks[me_x * gy + lax.rem(me_y + gy - 1, gy)]
    ahead = chunks[me_x * gy + lax.rem(me_y + 1, gy)]

    for number, ref, sigma, scale in (
        (1, ct, -1, time_step * section_b),
        (0, st, 1, time_step),
    ):
        lift = jnp.float32(lift_half * scale)
        wall = [
            jnp.where(rows < 2, reflect * lift, 0.0),
            jnp.where(rows >= 6, reflect * lift, 0.0),
        ]
        first_lane = jnp.where(lanes == 0, lift, 0.0)
        last_lane = jnp.where(lanes == LANES - 1, lift, 0.0)
        for b in (0, 3, 1, 2):
            for a in range(4):
                press = [load(ref, 0, a, b, h) for h in range(2)]
                vertical = [load(ref, 3, a, b, h) for h in range(2)]
                traces = wall_traces(press, vertical, sigma)
                for half in range(2):
                    term = wall[half] * traces[half]
                    plus = (sigma > 0) == (half == 0)
                    outs = {0: term, 3: term if plus else -term}
                    if b in (0, 3):
                        near = []
                        for part in range(3):
                            k = (number * 3 + part) * 8 + a * 2 + half
                            if b == 0:
                                near.append(first_lane * lane_roll(below, -k))
                            else:
                                near.append(last_lane * lane_roll(ahead, LANES - 1 - k))
                        outs[0] = outs[0] + near[0]
                        plus = (sigma > 0) == (b == 0)
                        outs[2] = near[0] if plus else -near[0]
                        outs[1] = near[1]
                        outs[3] = outs[3] + near[2]
                    at = rows_at(b, half)
                    for field, more in outs.items():
                        if number == 0:
                            full_rg[field, a, at, :] = new_rg[field, a, at, :] + more
                            full_st[field, a, at, :] = (
                                new_st[field, a, at, :] + jnp.float32(section_b) * more
                            )
                        else:
                            full_grad[field, a, at, :] = grad[field, a, at, :] + more
            if number == 0:
                store_lines(full_rg, rg_out, b, 1)
                store_lines(full_st, st_out, b, 0)
            else:
                store_lines(full_grad, grad_out, b, 2)
    for copy in stores:
        copy.wait()
    send_sum.wait()


def per_device(state, register, cotangent, impedance, wall_patch):
    gx, gy = lax.axis_size("gx"), lax.axis_size("gy")
    flat = (4, 4, 64, LANES)
    st, rg, ct = (v.reshape(flat) for v in (state, register, cotangent))
    imp = impedance.reshape(4, LANES)
    wp = wall_patch.reshape(4, LANES)
    f32 = jnp.float32
    any_place = pl.BlockSpec(memory_space=pltpu.HBM)
    on_chip = pl.BlockSpec(memory_space=pltpu.VMEM)
    whole = pltpu.VMEM(flat, f32)
    params = pltpu.CompilerParams(vmem_limit_bytes=8 * 2**20)
    halo = pltpu.VMEM((192, LANES), f32)
    st, ct, imp, wp, first, second, chunks = pl.pallas_call(
        functools.partial(pack_kernel, gx, gy),
        in_specs=[any_place] * 4,
        out_specs=[on_chip] * 7,
        out_shape=(
            whole,
            whole,
            pltpu.VMEM((4, LANES), f32),
            pltpu.VMEM((4, LANES), jnp.int32),
            halo,
            halo,
            pltpu.VMEM((gx * gy, 8, LANES), f32),
        ),
        scratch_shapes=[
            pltpu.SemaphoreType.DMA((2, 4)),
            pltpu.SemaphoreType.DMA((2,)),
            pltpu.VMEM((LANES, 4 * LANES), jnp.bfloat16),
        ],
        compiler_params=params,
        name="pack",
    )(*(pltpu.with_memory_space_constraint(v, pltpu.HBM) for v in (st, ct, imp, wp)))
    near = [(i, i ^ 1) for i in range(gx)]
    far = [(i, (i + 1) % gx if i % 2 else (i - 1) % gx) for i in range(gx)]
    first = lax.ppermute(first, "gx", near)
    second = lax.ppermute(second, "gx", far)
    chunks = lax.all_to_all(chunks, ("gx", "gy"), 0, 0)
    result = pltpu.HBM(flat, f32)
    new_st, new_rg, grad, st_out, rg_out, grad_out = pl.pallas_call(
        interior_kernel,
        in_specs=[on_chip] * 4 + [any_place],
        out_specs=[on_chip] * 3 + [any_place] * 3,
        out_shape=(whole, whole, whole, result, result, result),
        scratch_shapes=[pltpu.VMEM(flat, f32), pltpu.SemaphoreType.DMA((4,))],
        compiler_params=params,
        cost_estimate=pl.CostEstimate(
            flops=INTERIOR_FLOPS, bytes_accessed=2400000, transcendentals=0
        ),
        name="interior",
    )(st, ct, first, second, pltpu.with_memory_space_constraint(rg, pltpu.HBM))
    new_st, new_rg, grad, imp_grad = pl.pallas_call(
        functools.partial(finish_kernel, gx, gy),
        in_specs=[on_chip] * 8 + [any_place] * 3,
        out_specs=[any_place] * 4,
        out_shape=(result, result, result, pltpu.HBM((4, LANES), f32)),
        input_output_aliases={8: 0, 9: 1, 10: 2},
        scratch_shapes=[
            pltpu.VMEM((4 * gy, LANES), f32),
            pltpu.VMEM((4, LANES), f32),
            pltpu.VMEM(flat, f32),
            pltpu.VMEM(flat, f32),
            pltpu.VMEM(flat, f32),
            pltpu.SemaphoreType.DMA((3, 4)),
            pltpu.SemaphoreType.DMA((1,)),
        ],
        compiler_params=params,
        name="finish",
    )(st, ct, imp, wp, new_st, new_rg, grad, chunks, st_out, rg_out, grad_out)
    return (
        new_st.reshape(state.shape),
        new_rg.reshape(state.shape),
        grad.reshape(state.shape),
        imp_grad.reshape(impedance.shape),
    )


def solution(mesh):
    fields = P(None, None, None, "gx", "gy")
    return jax.shard_map(
        per_device,
        mesh=mesh,
        in_specs=(fields, fields, fields, P("gy"), P(None, "gx", "gy")),
        out_specs=(fields, fields, fields, P("gy")),
        check_vma=False,
    )
```

```python
import functools
import math

import jax
import jax.numpy as jnp
import numpy as np
from jax import lax
from jax.experimental import pallas as pl
from jax.experimental.pallas import tpu as pltpu
from jax.sharding import PartitionSpec as P

time_step = 0.02
section_a = -0.4178904745
section_b = 0.3792103129
lift_half = 6.0

LANES = 128
ROWS = 5


def derivative_table():
    points = np.array([-1.0, -1.0 / math.sqrt(5.0), 1.0 / math.sqrt(5.0), 1.0])
    identity = np.eye(4)
    distance = points[:, None] - points[None, :] + identity
    barycentric = 1.0 / np.prod(distance, axis=1)
    matrix = barycentric[None, :] / (barycentric[:, None] * distance)
    matrix = matrix * (1.0 - identity)
    matrix = matrix - identity * matrix.sum(axis=1)[:, None]
    return 2.0 * matrix


def rows_at(b, half):
    return pl.ds(b * 16 + half * 8, 8)


def load(ref, field, a, b, half):
    return ref[field, a, rows_at(b, half), :]


INTERIOR_FLOPS = 30000000000


def sub_roll(value, shift):
    return pltpu.roll(value, shift % 8, 0)


def lane_roll(value, shift):
    shift = shift % LANES
    return value if shift == 0 else pltpu.roll(value, shift, 1)


def rows_iota():
    return lax.broadcasted_iota(jnp.int32, (8, LANES), 0)


def lanes_iota():
    return lax.broadcasted_iota(jnp.int32, (8, LANES), 1)


def x_trace(ref, sigma, a, b, half):
    flip = sigma if a == 3 else -sigma
    press, normal = load(ref, 0, a, b, half), load(ref, 1, a, b, half)
    mixed = press + normal if flip > 0 else press - normal
    return [mixed, load(ref, 2, a, b, half), load(ref, 3, a, b, half)]


def y_trace(ref, sigma, a, b, half):
    flip = sigma if b == 3 else -sigma
    press, normal = load(ref, 0, a, b, half), load(ref, 2, a, b, half)
    mixed = press + normal if flip > 0 else press - normal
    return [mixed, load(ref, 1, a, b, half), load(ref, 3, a, b, half)]


def pack_kernel(
    gx,
    gy,
    st_in,
    ct_in,
    imp_in,
    wp_in,
    st,
    ct,
    imp,
    wp,
    first,
    second,
    third,
    fourth,
    chunks_out,
    chunks,
    one_hot,
    sems,
    small,
):
    me_x, me_y = lax.axis_index("gx"), lax.axis_index("gy")
    rows, lanes = rows_iota(), lanes_iota()
    even_row = (rows & 1) == 0
    even_me = (me_x & 1) == 0
    load_wp = pltpu.make_async_copy(wp_in, wp, small.at[0])
    load_wp.start()
    loads = {}
    for field in (0, 3, 2, 1):
        for number, (source, target) in enumerate(((st_in, st), (ct_in, ct))):
            loads[number, field] = pltpu.make_async_copy(
                source.at[field], target.at[field], sems.at[number, field]
            )
            loads[number, field].start()
    load_imp = pltpu.make_async_copy(imp_in, imp, small.at[1])
    load_imp.start()

    load_wp.wait()
    groups = 4 * gy
    count = 4 * LANES
    patch = jnp.concatenate([wp[r : r + 1, :] for r in range(4)], axis=1)
    high_of = lax.shift_right_logical(patch, 7)
    low_of = patch & (LANES - 1)
    hot = lax.broadcasted_iota(jnp.int32, (LANES, count), 0) == low_of
    one_hot[...] = jnp.where(hot, 1.0, 0.0).astype(jnp.bfloat16)

    for field in (0, 3):
        for number in range(2):
            loads[number, field].wait()
    floor = jnp.zeros((8, LANES), jnp.float32)
    ceil = jnp.zeros((8, LANES), jnp.float32)
    for a in range(4):
        for b in range(4):
            floor += (load(st, 0, a, b, 0) - load(st, 3, a, b, 0)) * (
                load(ct, 0, a, b, 0) + load(ct, 3, a, b, 0)
            )
            ceil += (load(st, 0, a, b, 1) + load(st, 3, a, b, 1)) * (
                load(ct, 0, a, b, 1) - load(ct, 3, a, b, 1)
            )
    values = jnp.concatenate([floor[0:1], floor[1:2], ceil[6:7], ceil[7:8]], axis=1)
    chosen = lax.broadcasted_iota(jnp.int32, (groups, count), 0) == high_of
    spread = jnp.where(chosen, jnp.broadcast_to(values, (groups, count)), 0.0)
    top = spread.astype(jnp.bfloat16)
    rest = spread - top.astype(jnp.float32)
    middle = rest.astype(jnp.bfloat16)
    last = (rest - middle.astype(jnp.float32)).astype(jnp.bfloat16)
    pieces = jnp.concatenate([top, middle, last], axis=0)
    sums = lax.dot_general(
        pieces, one_hot[...], (((1,), (1,)), ((), ())), preferred_element_type=jnp.float32
    )
    sums = sums[:groups] + sums[groups : 2 * groups] + sums[2 * groups :]
    load_imp.wait()
    width = LANES * 4 // gx
    per_row = gx // 4
    line = imp[pl.ds(me_x // per_row, 1), :]
    place = lax.rem(me_x, per_row)
    line_lanes = lax.broadcasted_iota(jnp.int32, (1, LANES), 1)
    line = jnp.where(line_lanes // width == place, line, 0.0)
    for target in range(gy):
        tile = jnp.concatenate([sums[target * 4 : target * 4 + 4], line], axis=0)
        for x in range(gx):
            chunks[pl.ds((x * gy + target) * ROWS, ROWS), :] = tile
    send = pltpu.make_async_copy(chunks, chunks_out, small.at[2])
    send.start()

    for field in (2, 1):
        for number in range(2):
            loads[number, field].wait()
    up = jnp.zeros((8, LANES), jnp.float32)
    down = jnp.zeros((8, LANES), jnp.float32)
    for number, (ref, sigma) in enumerate(((st, 1), (ct, -1))):
        for a in range(4):
            for half in range(2):
                high = y_trace(ref, sigma, a, 3, half)
                low = y_trace(ref, sigma, a, 0, half)
                for part in range(3):
                    k = (number * 3 + part) * 8 + a * 2 + half
                    up = jnp.where(lanes == k, lane_roll(high[part], k - 127), up)
                    down = jnp.where(lanes == k, lane_roll(low[part], k), down)
    even_me_y = (me_y & 1) == 0
    third[...] = jnp.where(even_me_y, up, down)
    fourth[...] = jnp.where(even_me_y, down, up)

    for number, (ref, sigma) in enumerate(((st, 1), (ct, -1))):
        for b in range(4):
            high = [x_trace(ref, sigma, 3, b, half) for half in range(2)]
            low = [x_trace(ref, sigma, 0, b, half) for half in range(2)]
            for part in range(3):
                to_right = jnp.where(even_row, sub_roll(high[0][part], -1), high[1][part])
                to_left = jnp.where(even_row, low[1][part], sub_roll(low[0][part], 1))
                at = pl.ds(((number * 3 + part) * 4 + b) * 8, 8)
                first[at, :] = jnp.where(even_me, to_right, to_left)
                second[at, :] = jnp.where(even_me, to_left, to_right)
    send.wait()


def interior(ref, sigma, matrix, scale, x_low, x_high, emit):
    rows = rows_iota()
    lower = rows < 4
    m = matrix * scale

    def pair(first, second):
        return jnp.where(lower, jnp.float32(first), jnp.float32(second))

    to_low = [pair(m[0, 1], m[1, 0]), pair(m[0, 2], m[1, 3]), pair(m[0, 3], m[1, 2])]
    to_high = [pair(m[2, 0], m[3, 1]), pair(m[2, 1], m[3, 0]), pair(m[2, 3], m[3, 2])]
    lift = jnp.float32(lift_half * scale)
    six = [
        jnp.where((rows >= 2) & (rows < 4), lift, 0.0),
        jnp.where((rows >= 4) & (rows < 6), lift, 0.0),
    ]
    z_face = [lower, rows >= 4]
    lanes = lanes_iota()
    even_row = (rows & 1) == 0

    def own(count, half, inner_only):
        face = (six[half] > 0.0) if inner_only else z_face[half]
        return jnp.where(face, -lift * (count + 1), -lift * count)

    diagonal = {
        (count, half, inner): own(count, half, inner)
        for count in range(3)
        for half in range(2)
        for inner in (False, True)
    }

    def weighted(field, fixed, index, axis):
        total = None
        for other in range(4):
            if other == index:
                continue
            a, b, half = fixed
            if axis == 0:
                a = other
            else:
                b = other
            term = jnp.float32(m[index, other]) * load(ref, field, a, b, half)
            total = term if total is None else total + term
        return total

    def c_weighted(values, rolled, half):
        if half == 0:
            return to_low[0] * rolled[0] + to_low[1] * values[1] + to_low[2] * rolled[1]
        return to_high[0] * values[0] + to_high[1] * rolled[0] + to_high[2] * rolled[1]

    for a in range(4):
        for b in range(4):
            press = [load(ref, 0, a, b, h) for h in range(2)]
            vel = [[load(ref, 1 + i, a, b, h) for h in range(2)] for i in range(3)]
            press_rolled = [sub_roll(v, 4) for v in press]
            up_rolled = [sub_roll(v, 4) for v in vel[2]]
            e0, e1 = wall_traces(press, vel[2], sigma)
            z_terms = [six[0] * sub_roll(e1, -2), six[1] * sub_roll(e0, 2)]
            count = (1 if a in (0, 3) else 0) + (1 if b in (0, 3) else 0)
            for half in range(2):
                fixed = (a, b, half)
                out_p = (
                    weighted(1, fixed, a, 0)
                    + weighted(2, fixed, b, 1)
                    + c_weighted(vel[2], up_rolled, half)
                )
                out_1 = weighted(0, fixed, a, 0)
                out_2 = weighted(0, fixed, b, 1)
                out_3 = c_weighted(press, press_rolled, half)
                out_p = out_p + diagonal[count, half, False] * press[half] + z_terms[half]
                out_1 = out_1 + diagonal[count, half, True] * vel[0][half]
                out_2 = out_2 + diagonal[count, half, True] * vel[1][half]
                out_3 = out_3 + diagonal[count, half, False] * vel[2][half]
                plus = (sigma > 0) == (half == 0)
                out_3 = out_3 + z_terms[half] if plus else out_3 - z_terms[half]
                turn = -2 if half == 0 else 2
                out_1 = out_1 + six[half] * sub_roll(vel[0][1 - half], turn)
                out_2 = out_2 + six[half] * sub_roll(vel[1][1 - half], turn)
                if a in (0, 3):
                    theirs = x_trace(ref, sigma, 3 - a, b, half)
                    if a == 0:
                        near = [
                            jnp.where(even_row, x_low(part, b, half), sub_roll(t, 1))
                            for part, t in enumerate(theirs)
                        ]
                    else:
                        near = [
                            jnp.where(even_row, sub_roll(t, -1), x_high(part, b, half))
                            for part, t in enumerate(theirs)
                        ]
                    near = [lift * n for n in near]
                    out_p = out_p + near[0]
                    plus = (sigma > 0) == (a == 0)
                    out_1 = out_1 + near[0] if plus else out_1 - near[0]
                    out_2 = out_2 + near[1]
                    out_3 = out_3 + near[2]
                if b in (0, 3):
                    theirs = y_trace(ref, sigma, a, 3 - b, half)
                    if b == 0:
                        weight = jnp.where(lanes == 0, 0.0, lift)
                        near = [weight * lane_roll(t, 1) for t in theirs]
                    else:
                        weight = jnp.where(lanes == 127, 0.0, lift)
                        near = [weight * lane_roll(t, -1) for t in theirs]
                    out_p = out_p + near[0]
                    plus = (sigma > 0) == (b == 0)
                    out_2 = out_2 + near[0] if plus else out_2 - near[0]
                    out_1 = out_1 + near[1]
                    out_3 = out_3 + near[2]
                emit(a, b, half, (out_p, out_1, out_2, out_3))


def wall_traces(press, vertical, sigma):
    if sigma > 0:
        return press[0] - vertical[0], press[1] + vertical[1]
    return press[0] + vertical[0], press[1] - vertical[1]


def interior_kernel(
    st, ct, first, second, rg_in, new_st, new_rg, grad, st_out, rg_out, grad_out, rg, sems
):
    me_x = lax.axis_index("gx")
    load_rg = pltpu.make_async_copy(rg_in, rg, sems.at[3])
    load_rg.start()
    even_me = (me_x & 1) == 0

    def halos(number):
        def at(part, b):
            return pl.ds(((number * 3 + part) * 4 + b) * 8, 8)

        def x_low(part, b, half):
            got = jnp.where(even_me, second[at(part, b), :], first[at(part, b), :])
            return got if half == 0 else sub_roll(got, -1)

        def x_high(part, b, half):
            got = jnp.where(even_me, first[at(part, b), :], second[at(part, b), :])
            return got if half == 0 else sub_roll(got, 1)

        return x_low, x_high

    matrix = derivative_table()
    matrix = matrix * (1.0 - np.eye(4))

    def store(source, target, kind):
        inner = (pl.ds(1, 2), slice(None), pl.ds(16, 32))
        copy = pltpu.make_async_copy(source.at[inner], target.at[inner], sems.at[kind])
        copy.start()
        return copy

    def emit_grad(a, b, half, outs):
        at = rows_at(b, half)
        for field in range(4):
            grad[field, a, at, :] = ct[field, a, at, :] + outs[field]

    def emit_state(a, b, half, outs):
        at = rows_at(b, half)
        for field in range(4):
            following = jnp.float32(section_a) * rg[field, a, at, :] + outs[field]
            new_rg[field, a, at, :] = following
            new_st[field, a, at, :] = st[field, a, at, :] + jnp.float32(section_b) * following

    interior(ct, -1, -matrix.T, time_step * section_b, *halos(1), emit_grad)
    stores = [store(grad, grad_out, 2)]
    load_rg.wait()
    interior(st, 1, -matrix, time_step, *halos(0), emit_state)
    stores += [store(new_st, st_out, 0), store(new_rg, rg_out, 1)]
    for copy in stores:
        copy.wait()


def finish_kernel(
    gx,
    gy,
    st,
    ct,
    imp,
    wp,
    new_st,
    new_rg,
    grad,
    chunks,
    third,
    fourth,
    st_prior,
    rg_prior,
    grad_prior,
    st_out,
    rg_out,
    grad_out,
    imp_out,
    table,
    imp_grad,
    full_st,
    full_rg,
    full_grad,
    sems,
    last_sem,
):
    del st_prior, rg_prior, grad_prior
    me_y = lax.axis_index("gy")
    rows, lanes = rows_iota(), lanes_iota()
    stores = []

    def store(source, target, at, kind, piece):
        copy = pltpu.make_async_copy(source.at[at], target.at[at], sems.at[kind, piece])
        copy.start()
        stores.append(copy)

    def store_lines(source, target, b, kind):
        every = slice(None)
        if b in (0, 3):
            store(source, target, (every, every, pl.ds(b * 16, 16)), kind, b)
        if b == 2:
            for piece, field in ((1, 0), (2, 3)):
                at = (pl.ds(field, 1), every, pl.ds(16, 32))
                store(source, target, at, kind, piece)

    total = None
    per_row = gx // 4
    for y in range(gy):
        for quarter in range(4):
            parts = []
            for x in range(quarter * per_row, (quarter + 1) * per_row):
                start = (x * gy + y) * ROWS
                piece = chunks[start : start + 4, :]
                total = piece if total is None else total + piece
                parts.append(chunks[start + 4 : start + 5, :])
            line = functools.reduce(jnp.add, parts)
            table[y * 4 + quarter : y * 4 + quarter + 1, :] = (line - 1.0) / (line + 1.0)
    patch_sum = total
    above = imp[...] + 1.0
    factor = time_step * section_b * lift_half * 2.0
    imp_grad[...] = patch_sum * jnp.float32(factor) / (above * above)
    send_sum = pltpu.make_async_copy(imp_grad, imp_out, last_sem.at[0])
    send_sum.start()
    patch = jnp.concatenate([wp[...], wp[...]], axis=0)
    low_of = patch & (LANES - 1)
    high_of = lax.shift_right_logical(patch, 7)
    reflect = jnp.zeros((8, LANES), jnp.float32)
    for high in range(4 * gy):
        line = jnp.broadcast_to(table[high : high + 1, :], (8, LANES))
        found = jnp.take_along_axis(line, low_of, axis=1)
        reflect = jnp.where(high_of == high, found, reflect)

    even_me_y = (me_y & 1) == 0
    below = jnp.where(even_me_y, fourth[...], third[...])
    ahead = jnp.where(even_me_y, third[...], fourth[...])

    for number, ref, sigma, scale in (
        (1, ct, -1, time_step * section_b),
        (0, st, 1, time_step),
    ):
        lift = jnp.float32(lift_half * scale)
        wall = [
            jnp.where(rows < 2, reflect * lift, 0.0),
            jnp.where(rows >= 6, reflect * lift, 0.0),
        ]
        first_lane = jnp.where(lanes == 0, lift, 0.0)
        last_lane = jnp.where(lanes == LANES - 1, lift, 0.0)
        for b in (0, 3, 1, 2):
            for a in range(4):
                press = [load(ref, 0, a, b, h) for h in range(2)]
                vertical = [load(ref, 3, a, b, h) for h in range(2)]
                traces = wall_traces(press, vertical, sigma)
                for half in range(2):
                    term = wall[half] * traces[half]
                    plus = (sigma > 0) == (half == 0)
                    outs = {0: term, 3: term if plus else -term}
                    if b in (0, 3):
                        near = []
                        for part in range(3):
                            k = (number * 3 + part) * 8 + a * 2 + half
                            if b == 0:
                                near.append(first_lane * lane_roll(below, -k))
                            else:
                                near.append(last_lane * lane_roll(ahead, LANES - 1 - k))
                        outs[0] = outs[0] + near[0]
                        plus = (sigma > 0) == (b == 0)
                        outs[2] = near[0] if plus else -near[0]
                        outs[1] = near[1]
                        outs[3] = outs[3] + near[2]
                    at = rows_at(b, half)
                    for field, more in outs.items():
                        if number == 0:
                            full_rg[field, a, at, :] = new_rg[field, a, at, :] + more
                            full_st[field, a, at, :] = (
                                new_st[field, a, at, :] + jnp.float32(section_b) * more
                            )
                        else:
                            full_grad[field, a, at, :] = grad[field, a, at, :] + more
            if number == 0:
                store_lines(full_rg, rg_out, b, 1)
                store_lines(full_st, st_out, b, 0)
            else:
                store_lines(full_grad, grad_out, b, 2)
    for copy in stores:
        copy.wait()
    send_sum.wait()


def per_device(state, register, cotangent, impedance, wall_patch):
    gx, gy = lax.axis_size("gx"), lax.axis_size("gy")
    flat = (4, 4, 64, LANES)
    st, rg, ct = (v.reshape(flat) for v in (state, register, cotangent))
    imp = impedance.reshape(4, LANES)
    wp = wall_patch.reshape(4, LANES)
    f32 = jnp.float32
    any_place = pl.BlockSpec(memory_space=pltpu.HBM)
    on_chip = pl.BlockSpec(memory_space=pltpu.VMEM)
    whole = pltpu.VMEM(flat, f32)
    params = pltpu.CompilerParams(vmem_limit_bytes=8 * 2**20)
    halo = pltpu.VMEM((192, LANES), f32)
    column = pltpu.VMEM((8, LANES), f32)
    st, ct, imp, wp, first, second, third, fourth, chunks = pl.pallas_call(
        functools.partial(pack_kernel, gx, gy),
        in_specs=[any_place] * 4,
        out_specs=[on_chip] * 8 + [any_place],
        out_shape=(
            whole,
            whole,
            pltpu.VMEM((4, LANES), f32),
            pltpu.VMEM((4, LANES), jnp.int32),
            halo,
            halo,
            column,
            column,
            pltpu.HBM((gx * gy * ROWS, LANES), f32),
        ),
        scratch_shapes=[
            pltpu.VMEM((gx * gy * ROWS, LANES), f32),
            pltpu.VMEM((LANES, 4 * LANES), jnp.bfloat16),
            pltpu.SemaphoreType.DMA((2, 4)),
            pltpu.SemaphoreType.DMA((3,)),
        ],
        compiler_params=params,
        name="pack",
    )(*(pltpu.with_memory_space_constraint(v, pltpu.HBM) for v in (st, ct, imp, wp)))

    def near(count):
        return [(i, i ^ 1) for i in range(count)]

    def far(count):
        return [(i, (i + 1) % count if i % 2 else (i - 1) % count) for i in range(count)]

    first = lax.ppermute(first, "gx", near(gx))
    second = lax.ppermute(second, "gx", far(gx))
    chunks = lax.all_to_all(
        chunks.reshape(gx * gy, ROWS, 1, LANES), ("gx", "gy"), 0, 0
    ).reshape(gx * gy * ROWS, LANES)
    third = lax.ppermute(third, "gy", near(gy))
    fourth = lax.ppermute(fourth, "gy", far(gy))
    result = pltpu.HBM(flat, f32)
    new_st, new_rg, grad, st_out, rg_out, grad_out = pl.pallas_call(
        interior_kernel,
        in_specs=[on_chip] * 4 + [any_place],
        out_specs=[on_chip] * 3 + [any_place] * 3,
        out_shape=(whole, whole, whole, result, result, result),
        scratch_shapes=[pltpu.VMEM(flat, f32), pltpu.SemaphoreType.DMA((4,))],
        compiler_params=params,
        cost_estimate=pl.CostEstimate(
            flops=INTERIOR_FLOPS, bytes_accessed=2400000, transcendentals=0
        ),
        name="interior",
    )(st, ct, first, second, pltpu.with_memory_space_constraint(rg, pltpu.HBM))
    new_st, new_rg, grad, imp_grad = pl.pallas_call(
        functools.partial(finish_kernel, gx, gy),
        in_specs=[on_chip] * 10 + [any_place] * 3,
        out_specs=[any_place] * 4,
        out_shape=(result, result, result, pltpu.HBM((4, LANES), f32)),
        input_output_aliases={10: 0, 11: 1, 12: 2},
        scratch_shapes=[
            pltpu.VMEM((4 * gy, LANES), f32),
            pltpu.VMEM((4, LANES), f32),
            pltpu.VMEM(flat, f32),
            pltpu.VMEM(flat, f32),
            pltpu.VMEM(flat, f32),
            pltpu.SemaphoreType.DMA((3, 4)),
            pltpu.SemaphoreType.DMA((1,)),
        ],
        compiler_params=params,
        name="finish",
    )(
        st,
        ct,
        imp,
        wp,
        new_st,
        new_rg,
        grad,
        chunks,
        third,
        fourth,
        st_out,
        rg_out,
        grad_out,
    )
    return (
        new_st.reshape(state.shape),
        new_rg.reshape(state.shape),
        grad.reshape(state.shape),
        imp_grad.reshape(impedance.shape),
    )


def solution(mesh):
    fields = P(None, None, None, "gx", "gy")
    return jax.shard_map(
        per_device,
        mesh=mesh,
        in_specs=(fields, fields, fields, P("gy"), P(None, "gx", "gy")),
        out_specs=(fields, fields, fields, P("gy")),
        check_vma=False,
    )
```

```python
import functools
import math

import jax
import jax.numpy as jnp
import numpy as np
from jax import lax
from jax.experimental import pallas as pl
from jax.experimental.pallas import tpu as pltpu
from jax.sharding import PartitionSpec as P

time_step = 0.02
section_a = -0.4178904745
section_b = 0.3792103129
lift_half = 6.0

LANES = 128
ROWS = 5


def derivative_table():
    points = np.array([-1.0, -1.0 / math.sqrt(5.0), 1.0 / math.sqrt(5.0), 1.0])
    identity = np.eye(4)
    distance = points[:, None] - points[None, :] + identity
    barycentric = 1.0 / np.prod(distance, axis=1)
    matrix = barycentric[None, :] / (barycentric[:, None] * distance)
    matrix = matrix * (1.0 - identity)
    matrix = matrix - identity * matrix.sum(axis=1)[:, None]
    return 2.0 * matrix


def group_order(gx, gy):
    return list(range(gx * gy))[::-1]


def slots_of(gx, gy):
    order = group_order(gx, gy)
    return [order.index(device) for device in range(gx * gy)]


def rows_at(b, half):
    return pl.ds(b * 16 + half * 8, 8)


def load(ref, field, a, b, half):
    return ref[field, a, rows_at(b, half), :]


INTERIOR_FLOPS = 30000000000


def sub_roll(value, shift):
    return pltpu.roll(value, shift % 8, 0)


def lane_roll(value, shift):
    shift = shift % LANES
    return value if shift == 0 else pltpu.roll(value, shift, 1)


def rows_iota():
    return lax.broadcasted_iota(jnp.int32, (8, LANES), 0)


def lanes_iota():
    return lax.broadcasted_iota(jnp.int32, (8, LANES), 1)


def x_trace(ref, sigma, a, b, half):
    flip = sigma if a == 3 else -sigma
    press, normal = load(ref, 0, a, b, half), load(ref, 1, a, b, half)
    mixed = press + normal if flip > 0 else press - normal
    return [mixed, load(ref, 2, a, b, half), load(ref, 3, a, b, half)]


def y_trace(ref, sigma, a, b, half):
    flip = sigma if b == 3 else -sigma
    press, normal = load(ref, 0, a, b, half), load(ref, 2, a, b, half)
    mixed = press + normal if flip > 0 else press - normal
    return [mixed, load(ref, 1, a, b, half), load(ref, 3, a, b, half)]


def pack_kernel(
    gx,
    gy,
    st_in,
    ct_in,
    imp_in,
    wp_in,
    st,
    ct,
    imp,
    wp,
    first,
    second,
    third,
    fourth,
    chunks_out,
    chunks,
    one_hot,
    sems,
    small,
):
    me_x, me_y = lax.axis_index("gx"), lax.axis_index("gy")
    rows, lanes = rows_iota(), lanes_iota()
    even_row = (rows & 1) == 0
    even_me = (me_x & 1) == 0
    load_wp = pltpu.make_async_copy(wp_in, wp, small.at[0])
    load_wp.start()
    loads = {}
    for field in (0, 3, 2, 1):
        for number, (source, target) in enumerate(((st_in, st), (ct_in, ct))):
            loads[number, field] = pltpu.make_async_copy(
                source.at[field], target.at[field], sems.at[number, field]
            )
            loads[number, field].start()
    load_imp = pltpu.make_async_copy(imp_in, imp, small.at[1])
    load_imp.start()

    load_wp.wait()
    groups = 4 * gy
    slots = slots_of(gx, gy)
    count = 4 * LANES
    patch = jnp.concatenate([wp[r : r + 1, :] for r in range(4)], axis=1)
    high_of = lax.shift_right_logical(patch, 7)
    low_of = patch & (LANES - 1)
    hot = lax.broadcasted_iota(jnp.int32, (LANES, count), 0) == low_of
    one_hot[...] = jnp.where(hot, 1.0, 0.0).astype(jnp.bfloat16)

    for field in (0, 3):
        for number in range(2):
            loads[number, field].wait()
    floor = jnp.zeros((8, LANES), jnp.float32)
    ceil = jnp.zeros((8, LANES), jnp.float32)
    for a in range(4):
        for b in range(4):
            floor += (load(st, 0, a, b, 0) - load(st, 3, a, b, 0)) * (
                load(ct, 0, a, b, 0) + load(ct, 3, a, b, 0)
            )
            ceil += (load(st, 0, a, b, 1) + load(st, 3, a, b, 1)) * (
                load(ct, 0, a, b, 1) - load(ct, 3, a, b, 1)
            )
    values = jnp.concatenate([floor[0:1], floor[1:2], ceil[6:7], ceil[7:8]], axis=1)
    chosen = lax.broadcasted_iota(jnp.int32, (groups, count), 0) == high_of
    spread = jnp.where(chosen, jnp.broadcast_to(values, (groups, count)), 0.0)
    top = spread.astype(jnp.bfloat16)
    rest = spread - top.astype(jnp.float32)
    middle = rest.astype(jnp.bfloat16)
    last = (rest - middle.astype(jnp.float32)).astype(jnp.bfloat16)
    pieces = jnp.concatenate([top, middle, last], axis=0)
    sums = lax.dot_general(
        pieces, one_hot[...], (((1,), (1,)), ((), ())), preferred_element_type=jnp.float32
    )
    sums = sums[:groups] + sums[groups : 2 * groups] + sums[2 * groups :]
    load_imp.wait()
    width = LANES * 4 // gx
    per_row = gx // 4
    line = imp[pl.ds(me_x // per_row, 1), :]
    place = lax.rem(me_x, per_row)
    line_lanes = lax.broadcasted_iota(jnp.int32, (1, LANES), 1)
    line = jnp.where(line_lanes // width == place, line, 0.0)
    for target in range(gy):
        tile = jnp.concatenate([sums[target * 4 : target * 4 + 4], line], axis=0)
        for x in range(gx):
            chunks[pl.ds(slots[x * gy + target] * ROWS, ROWS), :] = tile
    send = pltpu.make_async_copy(chunks, chunks_out, small.at[2])
    send.start()

    for field in (2, 1):
        for number in range(2):
            loads[number, field].wait()
    up = jnp.zeros((8, LANES), jnp.float32)
    down = jnp.zeros((8, LANES), jnp.float32)
    for number, (ref, sigma) in enumerate(((st, 1), (ct, -1))):
        for a in range(4):
            for half in range(2):
                high = y_trace(ref, sigma, a, 3, half)
                low = y_trace(ref, sigma, a, 0, half)
                for part in range(3):
                    k = (number * 3 + part) * 8 + a * 2 + half
                    up = jnp.where(lanes == k, lane_roll(high[part], k - 127), up)
                    down = jnp.where(lanes == k, lane_roll(low[part], k), down)
    even_me_y = (me_y & 1) == 0
    third[...] = jnp.where(even_me_y, up, down)
    fourth[...] = jnp.where(even_me_y, down, up)

    for number, (ref, sigma) in enumerate(((st, 1), (ct, -1))):
        for b in range(4):
            high = [x_trace(ref, sigma, 3, b, half) for half in range(2)]
            low = [x_trace(ref, sigma, 0, b, half) for half in range(2)]
            for part in range(3):
                to_right = jnp.where(even_row, sub_roll(high[0][part], -1), high[1][part])
                to_left = jnp.where(even_row, low[1][part], sub_roll(low[0][part], 1))
                at = pl.ds(((number * 3 + part) * 4 + b) * 8, 8)
                first[at, :] = jnp.where(even_me, to_right, to_left)
                second[at, :] = jnp.where(even_me, to_left, to_right)
    send.wait()


def interior(ref, sigma, matrix, scale, x_low, x_high, emit):
    rows = rows_iota()
    lower = rows < 4
    m = matrix * scale

    def pair(first, second):
        return jnp.where(lower, jnp.float32(first), jnp.float32(second))

    to_low = [pair(m[0, 1], m[1, 0]), pair(m[0, 2], m[1, 3]), pair(m[0, 3], m[1, 2])]
    to_high = [pair(m[2, 0], m[3, 1]), pair(m[2, 1], m[3, 0]), pair(m[2, 3], m[3, 2])]
    lift = jnp.float32(lift_half * scale)
    six = [
        jnp.where((rows >= 2) & (rows < 4), lift, 0.0),
        jnp.where((rows >= 4) & (rows < 6), lift, 0.0),
    ]
    z_face = [lower, rows >= 4]
    lanes = lanes_iota()
    even_row = (rows & 1) == 0

    def own(count, half, inner_only):
        face = (six[half] > 0.0) if inner_only else z_face[half]
        return jnp.where(face, -lift * (count + 1), -lift * count)

    diagonal = {
        (count, half, inner): own(count, half, inner)
        for count in range(3)
        for half in range(2)
        for inner in (False, True)
    }

    def weighted(field, fixed, index, axis):
        total = None
        for other in range(4):
            if other == index:
                continue
            a, b, half = fixed
            if axis == 0:
                a = other
            else:
                b = other
            term = jnp.float32(m[index, other]) * load(ref, field, a, b, half)
            total = term if total is None else total + term
        return total

    def c_weighted(values, rolled, half):
        if half == 0:
            return to_low[0] * rolled[0] + to_low[1] * values[1] + to_low[2] * rolled[1]
        return to_high[0] * values[0] + to_high[1] * rolled[0] + to_high[2] * rolled[1]

    for a in range(4):
        for b in range(4):
            press = [load(ref, 0, a, b, h) for h in range(2)]
            vel = [[load(ref, 1 + i, a, b, h) for h in range(2)] for i in range(3)]
            press_rolled = [sub_roll(v, 4) for v in press]
            up_rolled = [sub_roll(v, 4) for v in vel[2]]
            e0, e1 = wall_traces(press, vel[2], sigma)
            z_terms = [six[0] * sub_roll(e1, -2), six[1] * sub_roll(e0, 2)]
            count = (1 if a in (0, 3) else 0) + (1 if b in (0, 3) else 0)
            for half in range(2):
                fixed = (a, b, half)
                out_p = (
                    weighted(1, fixed, a, 0)
                    + weighted(2, fixed, b, 1)
                    + c_weighted(vel[2], up_rolled, half)
                )
                out_1 = weighted(0, fixed, a, 0)
                out_2 = weighted(0, fixed, b, 1)
                out_3 = c_weighted(press, press_rolled, half)
                out_p = out_p + diagonal[count, half, False] * press[half] + z_terms[half]
                out_1 = out_1 + diagonal[count, half, True] * vel[0][half]
                out_2 = out_2 + diagonal[count, half, True] * vel[1][half]
                out_3 = out_3 + diagonal[count, half, False] * vel[2][half]
                plus = (sigma > 0) == (half == 0)
                out_3 = out_3 + z_terms[half] if plus else out_3 - z_terms[half]
                turn = -2 if half == 0 else 2
                out_1 = out_1 + six[half] * sub_roll(vel[0][1 - half], turn)
                out_2 = out_2 + six[half] * sub_roll(vel[1][1 - half], turn)
                if a in (0, 3):
                    theirs = x_trace(ref, sigma, 3 - a, b, half)
                    if a == 0:
                        near = [
                            jnp.where(even_row, x_low(part, b, half), sub_roll(t, 1))
                            for part, t in enumerate(theirs)
                        ]
                    else:
                        near = [
                            jnp.where(even_row, sub_roll(t, -1), x_high(part, b, half))
                            for part, t in enumerate(theirs)
                        ]
                    near = [lift * n for n in near]
                    out_p = out_p + near[0]
                    plus = (sigma > 0) == (a == 0)
                    out_1 = out_1 + near[0] if plus else out_1 - near[0]
                    out_2 = out_2 + near[1]
                    out_3 = out_3 + near[2]
                if b in (0, 3):
                    theirs = y_trace(ref, sigma, a, 3 - b, half)
                    if b == 0:
                        weight = jnp.where(lanes == 0, 0.0, lift)
                        near = [weight * lane_roll(t, 1) for t in theirs]
                    else:
                        weight = jnp.where(lanes == 127, 0.0, lift)
                        near = [weight * lane_roll(t, -1) for t in theirs]
                    out_p = out_p + near[0]
                    plus = (sigma > 0) == (b == 0)
                    out_2 = out_2 + near[0] if plus else out_2 - near[0]
                    out_1 = out_1 + near[1]
                    out_3 = out_3 + near[2]
                emit(a, b, half, (out_p, out_1, out_2, out_3))


def wall_traces(press, vertical, sigma):
    if sigma > 0:
        return press[0] - vertical[0], press[1] + vertical[1]
    return press[0] + vertical[0], press[1] - vertical[1]


def interior_kernel(
    st, ct, first, second, rg_in, new_st, new_rg, grad, st_out, rg_out, grad_out, rg, sems
):
    me_x = lax.axis_index("gx")
    load_rg = pltpu.make_async_copy(rg_in, rg, sems.at[3])
    load_rg.start()
    even_me = (me_x & 1) == 0

    def halos(number):
        def at(part, b):
            return pl.ds(((number * 3 + part) * 4 + b) * 8, 8)

        def x_low(part, b, half):
            got = jnp.where(even_me, second[at(part, b), :], first[at(part, b), :])
            return got if half == 0 else sub_roll(got, -1)

        def x_high(part, b, half):
            got = jnp.where(even_me, first[at(part, b), :], second[at(part, b), :])
            return got if half == 0 else sub_roll(got, 1)

        return x_low, x_high

    matrix = derivative_table()
    matrix = matrix * (1.0 - np.eye(4))

    def store(source, target, kind):
        inner = (pl.ds(1, 2), slice(None), pl.ds(16, 32))
        copy = pltpu.make_async_copy(source.at[inner], target.at[inner], sems.at[kind])
        copy.start()
        return copy

    def emit_grad(a, b, half, outs):
        at = rows_at(b, half)
        for field in range(4):
            grad[field, a, at, :] = ct[field, a, at, :] + outs[field]

    def emit_state(a, b, half, outs):
        at = rows_at(b, half)
        for field in range(4):
            following = jnp.float32(section_a) * rg[field, a, at, :] + outs[field]
            new_rg[field, a, at, :] = following
            new_st[field, a, at, :] = st[field, a, at, :] + jnp.float32(section_b) * following

    interior(ct, -1, -matrix.T, time_step * section_b, *halos(1), emit_grad)
    stores = [store(grad, grad_out, 2)]
    load_rg.wait()
    interior(st, 1, -matrix, time_step, *halos(0), emit_state)
    stores += [store(new_st, st_out, 0), store(new_rg, rg_out, 1)]
    for copy in stores:
        copy.wait()


def finish_kernel(
    gx,
    gy,
    st,
    ct,
    imp,
    wp,
    new_st,
    new_rg,
    grad,
    chunks,
    third,
    fourth,
    st_prior,
    rg_prior,
    grad_prior,
    st_out,
    rg_out,
    grad_out,
    imp_out,
    table,
    imp_grad,
    full_st,
    full_rg,
    full_grad,
    sems,
    last_sem,
):
    del st_prior, rg_prior, grad_prior
    me_y = lax.axis_index("gy")
    rows, lanes = rows_iota(), lanes_iota()
    stores = []

    def store(source, target, at, kind, piece):
        copy = pltpu.make_async_copy(source.at[at], target.at[at], sems.at[kind, piece])
        copy.start()
        stores.append(copy)

    def store_lines(source, target, b, kind):
        every = slice(None)
        if b in (0, 3):
            store(source, target, (every, every, pl.ds(b * 16, 16)), kind, b)
        if b == 2:
            for piece, field in ((1, 0), (2, 3)):
                at = (pl.ds(field, 1), every, pl.ds(16, 32))
                store(source, target, at, kind, piece)

    slots = slots_of(gx, gy)
    total = None
    per_row = gx // 4
    for y in range(gy):
        for quarter in range(4):
            parts = []
            for x in range(quarter * per_row, (quarter + 1) * per_row):
                start = slots[x * gy + y] * ROWS
                piece = chunks[start : start + 4, :]
                total = piece if total is None else total + piece
                parts.append(chunks[start + 4 : start + 5, :])
            line = functools.reduce(jnp.add, parts)
            table[y * 4 + quarter : y * 4 + quarter + 1, :] = (line - 1.0) / (line + 1.0)
    patch_sum = total
    above = imp[...] + 1.0
    factor = time_step * section_b * lift_half * 2.0
    imp_grad[...] = patch_sum * jnp.float32(factor) / (above * above)
    send_sum = pltpu.make_async_copy(imp_grad, imp_out, last_sem.at[0])
    send_sum.start()
    patch = jnp.concatenate([wp[...], wp[...]], axis=0)
    low_of = patch & (LANES - 1)
    high_of = lax.shift_right_logical(patch, 7)
    reflect = jnp.zeros((8, LANES), jnp.float32)
    for high in range(4 * gy):
        line = jnp.broadcast_to(table[high : high + 1, :], (8, LANES))
        found = jnp.take_along_axis(line, low_of, axis=1)
        reflect = jnp.where(high_of == high, found, reflect)

    even_me_y = (me_y & 1) == 0
    below = jnp.where(even_me_y, fourth[...], third[...])
    ahead = jnp.where(even_me_y, third[...], fourth[...])

    for number, ref, sigma, scale in (
        (1, ct, -1, time_step * section_b),
        (0, st, 1, time_step),
    ):
        lift = jnp.float32(lift_half * scale)
        wall = [
            jnp.where(rows < 2, reflect * lift, 0.0),
            jnp.where(rows >= 6, reflect * lift, 0.0),
        ]
        first_lane = jnp.where(lanes == 0, lift, 0.0)
        last_lane = jnp.where(lanes == LANES - 1, lift, 0.0)
        for b in (0, 3, 1, 2):
            for a in range(4):
                press = [load(ref, 0, a, b, h) for h in range(2)]
                vertical = [load(ref, 3, a, b, h) for h in range(2)]
                traces = wall_traces(press, vertical, sigma)
                for half in range(2):
                    term = wall[half] * traces[half]
                    plus = (sigma > 0) == (half == 0)
                    outs = {0: term, 3: term if plus else -term}
                    if b in (0, 3):
                        near = []
                        for part in range(3):
                            k = (number * 3 + part) * 8 + a * 2 + half
                            if b == 0:
                                near.append(first_lane * lane_roll(below, -k))
                            else:
                                near.append(last_lane * lane_roll(ahead, LANES - 1 - k))
                        outs[0] = outs[0] + near[0]
                        plus = (sigma > 0) == (b == 0)
                        outs[2] = near[0] if plus else -near[0]
                        outs[1] = near[1]
                        outs[3] = outs[3] + near[2]
                    at = rows_at(b, half)
                    for field, more in outs.items():
                        if number == 0:
                            full_rg[field, a, at, :] = new_rg[field, a, at, :] + more
                            full_st[field, a, at, :] = (
                                new_st[field, a, at, :] + jnp.float32(section_b) * more
                            )
                        else:
                            full_grad[field, a, at, :] = grad[field, a, at, :] + more
            if number == 0:
                store_lines(full_rg, rg_out, b, 1)
                store_lines(full_st, st_out, b, 0)
            else:
                store_lines(full_grad, grad_out, b, 2)
    for copy in stores:
        copy.wait()
    send_sum.wait()


def per_device(state, register, cotangent, impedance, wall_patch):
    gx, gy = lax.axis_size("gx"), lax.axis_size("gy")
    flat = (4, 4, 64, LANES)
    st, rg, ct = (v.reshape(flat) for v in (state, register, cotangent))
    imp = impedance.reshape(4, LANES)
    wp = wall_patch.reshape(4, LANES)
    f32 = jnp.float32
    any_place = pl.BlockSpec(memory_space=pltpu.HBM)
    on_chip = pl.BlockSpec(memory_space=pltpu.VMEM)
    whole = pltpu.VMEM(flat, f32)
    params = pltpu.CompilerParams(vmem_limit_bytes=8 * 2**20)
    halo = pltpu.VMEM((192, LANES), f32)
    column = pltpu.VMEM((8, LANES), f32)
    st, ct, imp, wp, first, second, third, fourth, chunks = pl.pallas_call(
        functools.partial(pack_kernel, gx, gy),
        in_specs=[any_place] * 4,
        out_specs=[on_chip] * 8 + [any_place],
        out_shape=(
            whole,
            whole,
            pltpu.VMEM((4, LANES), f32),
            pltpu.VMEM((4, LANES), jnp.int32),
            halo,
            halo,
            column,
            column,
            pltpu.HBM((gx * gy * ROWS, LANES), f32),
        ),
        scratch_shapes=[
            pltpu.VMEM((gx * gy * ROWS, LANES), f32),
            pltpu.VMEM((LANES, 4 * LANES), jnp.bfloat16),
            pltpu.SemaphoreType.DMA((2, 4)),
            pltpu.SemaphoreType.DMA((3,)),
        ],
        compiler_params=params,
        name="pack",
    )(*(pltpu.with_memory_space_constraint(v, pltpu.HBM) for v in (st, ct, imp, wp)))

    def near(count):
        return [(i, i ^ 1) for i in range(count)]

    def far(count):
        return [(i, (i + 1) % count if i % 2 else (i - 1) % count) for i in range(count)]

    first = lax.ppermute(first, "gx", near(gx))
    second = lax.ppermute(second, "gx", far(gx))
    chunks = lax.all_to_all(
        chunks.reshape(gx * gy, ROWS, 1, LANES), ("gx", "gy"), 0, 0, axis_index_groups=[group_order(gx, gy)]
    ).reshape(gx * gy * ROWS, LANES)
    third = lax.ppermute(third, "gy", near(gy))
    fourth = lax.ppermute(fourth, "gy", far(gy))
    result = pltpu.HBM(flat, f32)
    new_st, new_rg, grad, st_out, rg_out, grad_out = pl.pallas_call(
        interior_kernel,
        in_specs=[on_chip] * 4 + [any_place],
        out_specs=[on_chip] * 3 + [any_place] * 3,
        out_shape=(whole, whole, whole, result, result, result),
        scratch_shapes=[pltpu.VMEM(flat, f32), pltpu.SemaphoreType.DMA((4,))],
        compiler_params=params,
        cost_estimate=pl.CostEstimate(
            flops=INTERIOR_FLOPS, bytes_accessed=2400000, transcendentals=0
        ),
        name="interior",
    )(st, ct, first, second, pltpu.with_memory_space_constraint(rg, pltpu.HBM))
    new_st, new_rg, grad, imp_grad = pl.pallas_call(
        functools.partial(finish_kernel, gx, gy),
        in_specs=[on_chip] * 10 + [any_place] * 3,
        out_specs=[any_place] * 4,
        out_shape=(result, result, result, pltpu.HBM((4, LANES), f32)),
        input_output_aliases={10: 0, 11: 1, 12: 2},
        scratch_shapes=[
            pltpu.VMEM((4 * gy, LANES), f32),
            pltpu.VMEM((4, LANES), f32),
            pltpu.VMEM(flat, f32),
            pltpu.VMEM(flat, f32),
            pltpu.VMEM(flat, f32),
            pltpu.SemaphoreType.DMA((3, 4)),
            pltpu.SemaphoreType.DMA((1,)),
        ],
        compiler_params=params,
        name="finish",
    )(
        st,
        ct,
        imp,
        wp,
        new_st,
        new_rg,
        grad,
        chunks,
        third,
        fourth,
        st_out,
        rg_out,
        grad_out,
    )
    return (
        new_st.reshape(state.shape),
        new_rg.reshape(state.shape),
        grad.reshape(state.shape),
        imp_grad.reshape(impedance.shape),
    )


def solution(mesh):
    fields = P(None, None, None, "gx", "gy")
    return jax.shard_map(
        per_device,
        mesh=mesh,
        in_specs=(fields, fields, fields, P("gy"), P(None, "gx", "gy")),
        out_specs=(fields, fields, fields, P("gy")),
        check_vma=False,
    )
```

```python
import functools
import math

import jax
import jax.numpy as jnp
import numpy as np
from jax import lax
from jax.experimental import pallas as pl
from jax.experimental.pallas import tpu as pltpu
from jax.sharding import PartitionSpec as P

time_step = 0.02
section_a = -0.4178904745
section_b = 0.3792103129
lift_half = 6.0

LANES = 128
ROWS = 5


def derivative_table():
    points = np.array([-1.0, -1.0 / math.sqrt(5.0), 1.0 / math.sqrt(5.0), 1.0])
    identity = np.eye(4)
    distance = points[:, None] - points[None, :] + identity
    barycentric = 1.0 / np.prod(distance, axis=1)
    matrix = barycentric[None, :] / (barycentric[:, None] * distance)
    matrix = matrix * (1.0 - identity)
    matrix = matrix - identity * matrix.sum(axis=1)[:, None]
    return 2.0 * matrix


def group_order(gx, gy):
    return list(range(gx * gy))[::-1]


def slots_of(gx, gy):
    order = group_order(gx, gy)
    return [order.index(device) for device in range(gx * gy)]


def rows_at(b, half):
    return pl.ds(b * 16 + half * 8, 8)


def load(ref, field, a, b, half):
    return ref[field, a, rows_at(b, half), :]


INTERIOR_FLOPS = 30000000000


def sub_roll(value, shift):
    return pltpu.roll(value, shift % 8, 0)


def lane_roll(value, shift):
    shift = shift % LANES
    return value if shift == 0 else pltpu.roll(value, shift, 1)


def rows_iota():
    return lax.broadcasted_iota(jnp.int32, (8, LANES), 0)


def lanes_iota():
    return lax.broadcasted_iota(jnp.int32, (8, LANES), 1)


def x_trace(ref, sigma, a, b, half):
    flip = sigma if a == 3 else -sigma
    press, normal = load(ref, 0, a, b, half), load(ref, 1, a, b, half)
    mixed = press + normal if flip > 0 else press - normal
    return [mixed, load(ref, 2, a, b, half), load(ref, 3, a, b, half)]


def y_trace(ref, sigma, a, b, half):
    flip = sigma if b == 3 else -sigma
    press, normal = load(ref, 0, a, b, half), load(ref, 2, a, b, half)
    mixed = press + normal if flip > 0 else press - normal
    return [mixed, load(ref, 1, a, b, half), load(ref, 3, a, b, half)]


def pack_kernel(
    gx,
    gy,
    st_in,
    ct_in,
    imp_in,
    wp_in,
    st,
    ct,
    imp,
    wp,
    first,
    second,
    third,
    fourth,
    chunks_out,
    chunks,
    one_hot,
    sems,
    small,
):
    me_x, me_y = lax.axis_index("gx"), lax.axis_index("gy")
    rows, lanes = rows_iota(), lanes_iota()
    even_row = (rows & 1) == 0
    even_me = (me_x & 1) == 0
    load_wp = pltpu.make_async_copy(wp_in, wp, small.at[0])
    load_wp.start()
    load_imp = pltpu.make_async_copy(imp_in, imp, small.at[1])
    load_imp.start()
    loads = {}
    for field in (0, 3, 2, 1):
        for number, (source, target) in enumerate(((st_in, st), (ct_in, ct))):
            loads[number, field] = pltpu.make_async_copy(
                source.at[field], target.at[field], sems.at[number, field]
            )
            loads[number, field].start()

    load_wp.wait()
    groups = 4 * gy
    slots = slots_of(gx, gy)
    count = 4 * LANES
    patch = jnp.concatenate([wp[r : r + 1, :] for r in range(4)], axis=1)
    high_of = lax.shift_right_logical(patch, 7)
    low_of = patch & (LANES - 1)
    hot = lax.broadcasted_iota(jnp.int32, (LANES, count), 0) == low_of
    one_hot[...] = jnp.where(hot, 1.0, 0.0).astype(jnp.bfloat16)

    for field in (0, 3):
        for number in range(2):
            loads[number, field].wait()
    floor = jnp.zeros((8, LANES), jnp.float32)
    ceil = jnp.zeros((8, LANES), jnp.float32)
    for a in range(4):
        for b in range(4):
            floor += (load(st, 0, a, b, 0) - load(st, 3, a, b, 0)) * (
                load(ct, 0, a, b, 0) + load(ct, 3, a, b, 0)
            )
            ceil += (load(st, 0, a, b, 1) + load(st, 3, a, b, 1)) * (
                load(ct, 0, a, b, 1) - load(ct, 3, a, b, 1)
            )
    values = jnp.concatenate([floor[0:1], floor[1:2], ceil[6:7], ceil[7:8]], axis=1)
    chosen = lax.broadcasted_iota(jnp.int32, (groups, count), 0) == high_of
    spread = jnp.where(chosen, jnp.broadcast_to(values, (groups, count)), 0.0)
    top = spread.astype(jnp.bfloat16)
    rest = spread - top.astype(jnp.float32)
    middle = rest.astype(jnp.bfloat16)
    last = (rest - middle.astype(jnp.float32)).astype(jnp.bfloat16)
    pieces = jnp.concatenate([top, middle, last], axis=0)
    sums = lax.dot_general(
        pieces, one_hot[...], (((1,), (1,)), ((), ())), preferred_element_type=jnp.float32
    )
    sums = sums[:groups] + sums[groups : 2 * groups] + sums[2 * groups :]
    load_imp.wait()
    width = LANES * 4 // gx
    per_row = gx // 4
    line = imp[pl.ds(me_x // per_row, 1), :]
    place = lax.rem(me_x, per_row)
    line_lanes = lax.broadcasted_iota(jnp.int32, (1, LANES), 1)
    line = jnp.where(line_lanes // width == place, line, 0.0)
    for target in range(gy):
        tile = jnp.concatenate([sums[target * 4 : target * 4 + 4], line], axis=0)
        for x in range(gx):
            chunks[pl.ds(slots[x * gy + target] * ROWS, ROWS), :] = tile
    send = pltpu.make_async_copy(chunks, chunks_out, small.at[2])
    send.start()

    for field in (2, 1):
        for number in range(2):
            loads[number, field].wait()
    up = jnp.zeros((8, LANES), jnp.float32)
    down = jnp.zeros((8, LANES), jnp.float32)
    for number, (ref, sigma) in enumerate(((st, 1), (ct, -1))):
        for a in range(4):
            for half in range(2):
                high = y_trace(ref, sigma, a, 3, half)
                low = y_trace(ref, sigma, a, 0, half)
                for part in range(3):
                    k = (number * 3 + part) * 8 + a * 2 + half
                    up = jnp.where(lanes == k, lane_roll(high[part], k - 127), up)
                    down = jnp.where(lanes == k, lane_roll(low[part], k), down)
    even_me_y = (me_y & 1) == 0
    third[...] = jnp.where(even_me_y, up, down)
    fourth[...] = jnp.where(even_me_y, down, up)

    for number, (ref, sigma) in enumerate(((st, 1), (ct, -1))):
        for b in range(4):
            high = [x_trace(ref, sigma, 3, b, half) for half in range(2)]
            low = [x_trace(ref, sigma, 0, b, half) for half in range(2)]
            for part in range(3):
                to_right = jnp.where(even_row, sub_roll(high[0][part], -1), high[1][part])
                to_left = jnp.where(even_row, low[1][part], sub_roll(low[0][part], 1))
                at = pl.ds(((number * 3 + part) * 4 + b) * 8, 8)
                first[at, :] = jnp.where(even_me, to_right, to_left)
                second[at, :] = jnp.where(even_me, to_left, to_right)
    send.wait()


def interior(ref, sigma, matrix, scale, x_low, x_high, emit):
    rows = rows_iota()
    lower = rows < 4
    m = matrix * scale

    def pair(first, second):
        return jnp.where(lower, jnp.float32(first), jnp.float32(second))

    to_low = [pair(m[0, 1], m[1, 0]), pair(m[0, 2], m[1, 3]), pair(m[0, 3], m[1, 2])]
    to_high = [pair(m[2, 0], m[3, 1]), pair(m[2, 1], m[3, 0]), pair(m[2, 3], m[3, 2])]
    lift = jnp.float32(lift_half * scale)
    six = [
        jnp.where((rows >= 2) & (rows < 4), lift, 0.0),
        jnp.where((rows >= 4) & (rows < 6), lift, 0.0),
    ]
    z_face = [lower, rows >= 4]
    lanes = lanes_iota()
    even_row = (rows & 1) == 0

    def own(count, half, inner_only):
        face = (six[half] > 0.0) if inner_only else z_face[half]
        return jnp.where(face, -lift * (count + 1), -lift * count)

    diagonal = {
        (count, half, inner): own(count, half, inner)
        for count in range(3)
        for half in range(2)
        for inner in (False, True)
    }

    def weighted(field, fixed, index, axis):
        total = None
        for other in range(4):
            if other == index:
                continue
            a, b, half = fixed
            if axis == 0:
                a = other
            else:
                b = other
            term = jnp.float32(m[index, other]) * load(ref, field, a, b, half)
            total = term if total is None else total + term
        return total

    def c_weighted(values, rolled, half):
        if half == 0:
            return to_low[0] * rolled[0] + to_low[1] * values[1] + to_low[2] * rolled[1]
        return to_high[0] * values[0] + to_high[1] * rolled[0] + to_high[2] * rolled[1]

    for a in range(4):
        for b in range(4):
            press = [load(ref, 0, a, b, h) for h in range(2)]
            vel = [[load(ref, 1 + i, a, b, h) for h in range(2)] for i in range(3)]
            press_rolled = [sub_roll(v, 4) for v in press]
            up_rolled = [sub_roll(v, 4) for v in vel[2]]
            e0, e1 = wall_traces(press, vel[2], sigma)
            z_terms = [six[0] * sub_roll(e1, -2), six[1] * sub_roll(e0, 2)]
            count = (1 if a in (0, 3) else 0) + (1 if b in (0, 3) else 0)
            for half in range(2):
                fixed = (a, b, half)
                out_p = (
                    weighted(1, fixed, a, 0)
                    + weighted(2, fixed, b, 1)
                    + c_weighted(vel[2], up_rolled, half)
                )
                out_1 = weighted(0, fixed, a, 0)
                out_2 = weighted(0, fixed, b, 1)
                out_3 = c_weighted(press, press_rolled, half)
                out_p = out_p + diagonal[count, half, False] * press[half] + z_terms[half]
                out_1 = out_1 + diagonal[count, half, True] * vel[0][half]
                out_2 = out_2 + diagonal[count, half, True] * vel[1][half]
                out_3 = out_3 + diagonal[count, half, False] * vel[2][half]
                plus = (sigma > 0) == (half == 0)
                out_3 = out_3 + z_terms[half] if plus else out_3 - z_terms[half]
                turn = -2 if half == 0 else 2
                out_1 = out_1 + six[half] * sub_roll(vel[0][1 - half], turn)
                out_2 = out_2 + six[half] * sub_roll(vel[1][1 - half], turn)
                if a in (0, 3):
                    theirs = x_trace(ref, sigma, 3 - a, b, half)
                    if a == 0:
                        near = [
                            jnp.where(even_row, x_low(part, b, half), sub_roll(t, 1))
                            for part, t in enumerate(theirs)
                        ]
                    else:
                        near = [
                            jnp.where(even_row, sub_roll(t, -1), x_high(part, b, half))
                            for part, t in enumerate(theirs)
                        ]
                    near = [lift * n for n in near]
                    out_p = out_p + near[0]
                    plus = (sigma > 0) == (a == 0)
                    out_1 = out_1 + near[0] if plus else out_1 - near[0]
                    out_2 = out_2 + near[1]
                    out_3 = out_3 + near[2]
                if b in (0, 3):
                    theirs = y_trace(ref, sigma, a, 3 - b, half)
                    if b == 0:
                        weight = jnp.where(lanes == 0, 0.0, lift)
                        near = [weight * lane_roll(t, 1) for t in theirs]
                    else:
                        weight = jnp.where(lanes == 127, 0.0, lift)
                        near = [weight * lane_roll(t, -1) for t in theirs]
                    out_p = out_p + near[0]
                    plus = (sigma > 0) == (b == 0)
                    out_2 = out_2 + near[0] if plus else out_2 - near[0]
                    out_1 = out_1 + near[1]
                    out_3 = out_3 + near[2]
                emit(a, b, half, (out_p, out_1, out_2, out_3))


def wall_traces(press, vertical, sigma):
    if sigma > 0:
        return press[0] - vertical[0], press[1] + vertical[1]
    return press[0] + vertical[0], press[1] - vertical[1]


def interior_kernel(
    st, ct, first, second, rg_in, new_st, new_rg, grad, st_out, rg_out, grad_out, rg, sems
):
    me_x = lax.axis_index("gx")
    load_rg = pltpu.make_async_copy(rg_in, rg, sems.at[3])
    load_rg.start()
    even_me = (me_x & 1) == 0

    def halos(number):
        def at(part, b):
            return pl.ds(((number * 3 + part) * 4 + b) * 8, 8)

        def x_low(part, b, half):
            got = jnp.where(even_me, second[at(part, b), :], first[at(part, b), :])
            return got if half == 0 else sub_roll(got, -1)

        def x_high(part, b, half):
            got = jnp.where(even_me, first[at(part, b), :], second[at(part, b), :])
            return got if half == 0 else sub_roll(got, 1)

        return x_low, x_high

    matrix = derivative_table()
    matrix = matrix * (1.0 - np.eye(4))

    def store(source, target, kind):
        inner = (pl.ds(1, 2), slice(None), pl.ds(16, 32))
        copy = pltpu.make_async_copy(source.at[inner], target.at[inner], sems.at[kind])
        copy.start()
        return copy

    def emit_grad(a, b, half, outs):
        at = rows_at(b, half)
        for field in range(4):
            grad[field, a, at, :] = ct[field, a, at, :] + outs[field]

    def emit_state(a, b, half, outs):
        at = rows_at(b, half)
        for field in range(4):
            following = jnp.float32(section_a) * rg[field, a, at, :] + outs[field]
            new_rg[field, a, at, :] = following
            new_st[field, a, at, :] = st[field, a, at, :] + jnp.float32(section_b) * following

    interior(ct, -1, -matrix.T, time_step * section_b, *halos(1), emit_grad)
    stores = [store(grad, grad_out, 2)]
    load_rg.wait()
    interior(st, 1, -matrix, time_step, *halos(0), emit_state)
    stores += [store(new_st, st_out, 0), store(new_rg, rg_out, 1)]
    for copy in stores:
        copy.wait()


def finish_kernel(
    gx,
    gy,
    st,
    ct,
    imp,
    wp,
    new_st,
    new_rg,
    grad,
    chunks,
    third,
    fourth,
    st_prior,
    rg_prior,
    grad_prior,
    st_out,
    rg_out,
    grad_out,
    imp_out,
    table,
    imp_grad,
    full_st,
    full_rg,
    full_grad,
    sems,
    last_sem,
):
    del st_prior, rg_prior, grad_prior
    me_y = lax.axis_index("gy")
    rows, lanes = rows_iota(), lanes_iota()
    stores = []

    def store(source, target, at, kind, piece):
        copy = pltpu.make_async_copy(source.at[at], target.at[at], sems.at[kind, piece])
        copy.start()
        stores.append(copy)

    def store_lines(source, target, b, kind):
        every = slice(None)
        if b in (0, 3):
            store(source, target, (every, every, pl.ds(b * 16, 16)), kind, b)
        if b == 2:
            for piece, field in ((1, 0), (2, 3)):
                at = (pl.ds(field, 1), every, pl.ds(16, 32))
                store(source, target, at, kind, piece)

    slots = slots_of(gx, gy)
    total = None
    per_row = gx // 4
    for y in range(gy):
        for quarter in range(4):
            parts = []
            for x in range(quarter * per_row, (quarter + 1) * per_row):
                start = slots[x * gy + y] * ROWS
                piece = chunks[start : start + 4, :]
                total = piece if total is None else total + piece
                parts.append(chunks[start + 4 : start + 5, :])
            line = functools.reduce(jnp.add, parts)
            table[y * 4 + quarter : y * 4 + quarter + 1, :] = line
    patch_sum = total
    above = imp[...] + 1.0
    factor = time_step * section_b * lift_half * 2.0
    imp_grad[...] = patch_sum * jnp.float32(factor) / (above * above)
    send_sum = pltpu.make_async_copy(imp_grad, imp_out, last_sem.at[0])
    send_sum.start()
    patch = jnp.concatenate([wp[...], wp[...]], axis=0)
    low_of = patch & (LANES - 1)
    high_of = lax.shift_right_logical(patch, 7)
    chosen = jnp.zeros((8, LANES), jnp.float32)
    for high in range(4 * gy):
        line = jnp.broadcast_to(table[high : high + 1, :], (8, LANES))
        found = jnp.take_along_axis(line, low_of, axis=1)
        chosen = jnp.where(high_of == high, found, chosen)

    even_me_y = (me_y & 1) == 0
    below = jnp.where(even_me_y, fourth[...], third[...])
    ahead = jnp.where(even_me_y, third[...], fourth[...])
    reflect = (chosen - 1.0) / (chosen + 1.0)

    for number, ref, sigma, scale in (
        (1, ct, -1, time_step * section_b),
        (0, st, 1, time_step),
    ):
        lift = jnp.float32(lift_half * scale)
        wall = [
            jnp.where(rows < 2, reflect * lift, 0.0),
            jnp.where(rows >= 6, reflect * lift, 0.0),
        ]
        first_lane = jnp.where(lanes == 0, lift, 0.0)
        last_lane = jnp.where(lanes == LANES - 1, lift, 0.0)
        for b in (0, 3, 1, 2):
            for a in range(4):
                press = [load(ref, 0, a, b, h) for h in range(2)]
                vertical = [load(ref, 3, a, b, h) for h in range(2)]
                traces = wall_traces(press, vertical, sigma)
                for half in range(2):
                    term = wall[half] * traces[half]
                    plus = (sigma > 0) == (half == 0)
                    outs = {0: term, 3: term if plus else -term}
                    if b in (0, 3):
                        near = []
                        for part in range(3):
                            k = (number * 3 + part) * 8 + a * 2 + half
                            if b == 0:
                                near.append(first_lane * lane_roll(below, -k))
                            else:
                                near.append(last_lane * lane_roll(ahead, LANES - 1 - k))
                        outs[0] = outs[0] + near[0]
                        plus = (sigma > 0) == (b == 0)
                        outs[2] = near[0] if plus else -near[0]
                        outs[1] = near[1]
                        outs[3] = outs[3] + near[2]
                    at = rows_at(b, half)
                    for field, more in outs.items():
                        if number == 0:
                            full_rg[field, a, at, :] = new_rg[field, a, at, :] + more
                            full_st[field, a, at, :] = (
                                new_st[field, a, at, :] + jnp.float32(section_b) * more
                            )
                        else:
                            full_grad[field, a, at, :] = grad[field, a, at, :] + more
            if number == 0:
                store_lines(full_rg, rg_out, b, 1)
                store_lines(full_st, st_out, b, 0)
            else:
                store_lines(full_grad, grad_out, b, 2)
    for copy in stores:
        copy.wait()
    send_sum.wait()


def per_device(state, register, cotangent, impedance, wall_patch):
    gx, gy = lax.axis_size("gx"), lax.axis_size("gy")
    flat = (4, 4, 64, LANES)
    st, rg, ct = (v.reshape(flat) for v in (state, register, cotangent))
    imp = impedance.reshape(4, LANES)
    wp = wall_patch.reshape(4, LANES)
    f32 = jnp.float32
    any_place = pl.BlockSpec(memory_space=pltpu.HBM)
    on_chip = pl.BlockSpec(memory_space=pltpu.VMEM)
    whole = pltpu.VMEM(flat, f32)
    params = pltpu.CompilerParams(vmem_limit_bytes=8 * 2**20)
    halo = pltpu.VMEM((192, LANES), f32)
    column = pltpu.VMEM((8, LANES), f32)
    st, ct, imp, wp, first, second, third, fourth, chunks = pl.pallas_call(
        functools.partial(pack_kernel, gx, gy),
        in_specs=[any_place] * 4,
        out_specs=[on_chip] * 8 + [any_place],
        out_shape=(
            whole,
            whole,
            pltpu.VMEM((4, LANES), f32),
            pltpu.VMEM((4, LANES), jnp.int32),
            halo,
            halo,
            column,
            column,
            pltpu.HBM((gx * gy * ROWS, LANES), f32),
        ),
        scratch_shapes=[
            pltpu.VMEM((gx * gy * ROWS, LANES), f32),
            pltpu.VMEM((LANES, 4 * LANES), jnp.bfloat16),
            pltpu.SemaphoreType.DMA((2, 4)),
            pltpu.SemaphoreType.DMA((3,)),
        ],
        compiler_params=params,
        name="pack",
    )(*(pltpu.with_memory_space_constraint(v, pltpu.HBM) for v in (st, ct, imp, wp)))

    def near(count):
        return [(i, i ^ 1) for i in range(count)]

    def far(count):
        return [(i, (i + 1) % count if i % 2 else (i - 1) % count) for i in range(count)]

    first = lax.ppermute(first, "gx", near(gx))
    second = lax.ppermute(second, "gx", far(gx))
    chunks = lax.all_to_all(
        chunks.reshape(gx * gy, ROWS, 1, LANES), ("gx", "gy"), 0, 0, axis_index_groups=[group_order(gx, gy)]
    ).reshape(gx * gy * ROWS, LANES)
    third = lax.ppermute(third, "gy", near(gy))
    fourth = lax.ppermute(fourth, "gy", far(gy))
    result = pltpu.HBM(flat, f32)
    new_st, new_rg, grad, st_out, rg_out, grad_out = pl.pallas_call(
        interior_kernel,
        in_specs=[on_chip] * 4 + [any_place],
        out_specs=[on_chip] * 3 + [any_place] * 3,
        out_shape=(whole, whole, whole, result, result, result),
        scratch_shapes=[pltpu.VMEM(flat, f32), pltpu.SemaphoreType.DMA((4,))],
        compiler_params=params,
        cost_estimate=pl.CostEstimate(
            flops=INTERIOR_FLOPS, bytes_accessed=2400000, transcendentals=0
        ),
        name="interior",
    )(st, ct, first, second, pltpu.with_memory_space_constraint(rg, pltpu.HBM))
    new_st, new_rg, grad, imp_grad = pl.pallas_call(
        functools.partial(finish_kernel, gx, gy),
        in_specs=[on_chip] * 10 + [any_place] * 3,
        out_specs=[any_place] * 4,
        out_shape=(result, result, result, pltpu.HBM((4, LANES), f32)),
        input_output_aliases={10: 0, 11: 1, 12: 2},
        scratch_shapes=[
            pltpu.VMEM((4 * gy, LANES), f32),
            pltpu.VMEM((4, LANES), f32),
            pltpu.VMEM(flat, f32),
            pltpu.VMEM(flat, f32),
            pltpu.VMEM(flat, f32),
            pltpu.SemaphoreType.DMA((3, 4)),
            pltpu.SemaphoreType.DMA((1,)),
        ],
        compiler_params=params,
        name="finish",
    )(
        st,
        ct,
        imp,
        wp,
        new_st,
        new_rg,
        grad,
        chunks,
        third,
        fourth,
        st_out,
        rg_out,
        grad_out,
    )
    return (
        new_st.reshape(state.shape),
        new_rg.reshape(state.shape),
        grad.reshape(state.shape),
        imp_grad.reshape(impedance.shape),
    )


def solution(mesh):
    fields = P(None, None, None, "gx", "gy")
    return jax.shard_map(
        per_device,
        mesh=mesh,
        in_specs=(fields, fields, fields, P("gy"), P(None, "gx", "gy")),
        out_specs=(fields, fields, fields, P("gy")),
        check_vma=False,
    )
```

```python
import functools
import math

import jax
import jax.numpy as jnp
import numpy as np
from jax import lax
from jax.experimental import pallas as pl
from jax.experimental.pallas import tpu as pltpu
from jax.sharding import PartitionSpec as P

time_step = 0.02
section_a = -0.4178904745
section_b = 0.3792103129
lift_half = 6.0

LANES = 128
ROWS = 5


def derivative_table():
    points = np.array([-1.0, -1.0 / math.sqrt(5.0), 1.0 / math.sqrt(5.0), 1.0])
    identity = np.eye(4)
    distance = points[:, None] - points[None, :] + identity
    barycentric = 1.0 / np.prod(distance, axis=1)
    matrix = barycentric[None, :] / (barycentric[:, None] * distance)
    matrix = matrix * (1.0 - identity)
    matrix = matrix - identity * matrix.sum(axis=1)[:, None]
    return 2.0 * matrix


def group_order(gx, gy):
    first = list(range(gx * gy))[::-1]
    return first[gx * gy // 2 :] + first[: gx * gy // 2]


def slots_of(gx, gy):
    order = group_order(gx, gy)
    return [order.index(device) for device in range(gx * gy)]


def rows_at(b, half):
    return pl.ds(b * 16 + half * 8, 8)


def load(ref, field, a, b, half):
    return ref[field, a, rows_at(b, half), :]


INTERIOR_FLOPS = 30000000000


def sub_roll(value, shift):
    return pltpu.roll(value, shift % 8, 0)


def lane_roll(value, shift):
    shift = shift % LANES
    return value if shift == 0 else pltpu.roll(value, shift, 1)


def rows_iota():
    return lax.broadcasted_iota(jnp.int32, (8, LANES), 0)


def lanes_iota():
    return lax.broadcasted_iota(jnp.int32, (8, LANES), 1)


def x_trace(ref, sigma, a, b, half):
    flip = sigma if a == 3 else -sigma
    press, normal = load(ref, 0, a, b, half), load(ref, 1, a, b, half)
    mixed = press + normal if flip > 0 else press - normal
    return [mixed, load(ref, 2, a, b, half), load(ref, 3, a, b, half)]


def y_trace(ref, sigma, a, b, half):
    flip = sigma if b == 3 else -sigma
    press, normal = load(ref, 0, a, b, half), load(ref, 2, a, b, half)
    mixed = press + normal if flip > 0 else press - normal
    return [mixed, load(ref, 1, a, b, half), load(ref, 3, a, b, half)]


def pack_kernel(
    gx,
    gy,
    st_in,
    ct_in,
    imp_in,
    wp_in,
    st,
    ct,
    imp,
    wp,
    first,
    second,
    third,
    fourth,
    chunks_out,
    chunks,
    one_hot,
    sems,
    small,
):
    me_x, me_y = lax.axis_index("gx"), lax.axis_index("gy")
    rows, lanes = rows_iota(), lanes_iota()
    even_row = (rows & 1) == 0
    even_me = (me_x & 1) == 0
    load_wp = pltpu.make_async_copy(wp_in, wp, small.at[0])
    load_wp.start()
    loads = {}
    for field in (0, 3, 2, 1):
        for number, (source, target) in enumerate(((st_in, st), (ct_in, ct))):
            loads[number, field] = pltpu.make_async_copy(
                source.at[field], target.at[field], sems.at[number, field]
            )
            loads[number, field].start()
    load_imp = pltpu.make_async_copy(imp_in, imp, small.at[1])
    load_imp.start()

    load_wp.wait()
    groups = 4 * gy
    slots = slots_of(gx, gy)
    count = 4 * LANES
    patch = jnp.concatenate([wp[r : r + 1, :] for r in range(4)], axis=1)
    high_of = lax.shift_right_logical(patch, 7)
    low_of = patch & (LANES - 1)
    hot = lax.broadcasted_iota(jnp.int32, (LANES, count), 0) == low_of
    one_hot[...] = jnp.where(hot, 1.0, 0.0).astype(jnp.bfloat16)

    for field in (0, 3):
        for number in range(2):
            loads[number, field].wait()
    floor = jnp.zeros((8, LANES), jnp.float32)
    ceil = jnp.zeros((8, LANES), jnp.float32)
    for a in range(4):
        for b in range(4):
            floor += (load(st, 0, a, b, 0) - load(st, 3, a, b, 0)) * (
                load(ct, 0, a, b, 0) + load(ct, 3, a, b, 0)
            )
            ceil += (load(st, 0, a, b, 1) + load(st, 3, a, b, 1)) * (
                load(ct, 0, a, b, 1) - load(ct, 3, a, b, 1)
            )
    values = jnp.concatenate([floor[0:1], floor[1:2], ceil[6:7], ceil[7:8]], axis=1)
    chosen = lax.broadcasted_iota(jnp.int32, (groups, count), 0) == high_of
    spread = jnp.where(chosen, jnp.broadcast_to(values, (groups, count)), 0.0)
    top = spread.astype(jnp.bfloat16)
    rest = spread - top.astype(jnp.float32)
    middle = rest.astype(jnp.bfloat16)
    last = (rest - middle.astype(jnp.float32)).astype(jnp.bfloat16)
    pieces = jnp.concatenate([top, middle, last], axis=0)
    sums = lax.dot_general(
        pieces, one_hot[...], (((1,), (1,)), ((), ())), preferred_element_type=jnp.float32
    )
    sums = sums[:groups] + sums[groups : 2 * groups] + sums[2 * groups :]
    load_imp.wait()
    width = LANES * 4 // gx
    per_row = gx // 4
    line = imp[pl.ds(me_x // per_row, 1), :]
    place = lax.rem(me_x, per_row)
    line_lanes = lax.broadcasted_iota(jnp.int32, (1, LANES), 1)
    line = jnp.where(line_lanes // width == place, line, 0.0)
    for target in range(gy):
        tile = jnp.concatenate([sums[target * 4 : target * 4 + 4], line], axis=0)
        for x in range(gx):
            chunks[pl.ds(slots[x * gy + target] * ROWS, ROWS), :] = tile
    send = pltpu.make_async_copy(chunks, chunks_out, small.at[2])
    send.start()

    for field in (2, 1):
        for number in range(2):
            loads[number, field].wait()
    up = jnp.zeros((8, LANES), jnp.float32)
    down = jnp.zeros((8, LANES), jnp.float32)
    for number, (ref, sigma) in enumerate(((st, 1), (ct, -1))):
        for a in range(4):
            for half in range(2):
                high = y_trace(ref, sigma, a, 3, half)
                low = y_trace(ref, sigma, a, 0, half)
                for part in range(3):
                    k = (number * 3 + part) * 8 + a * 2 + half
                    up = jnp.where(lanes == k, lane_roll(high[part], k - 127), up)
                    down = jnp.where(lanes == k, lane_roll(low[part], k), down)
    even_me_y = (me_y & 1) == 0
    third[...] = jnp.where(even_me_y, up, down)
    fourth[...] = jnp.where(even_me_y, down, up)

    for number, (ref, sigma) in enumerate(((st, 1), (ct, -1))):
        for b in range(4):
            high = [x_trace(ref, sigma, 3, b, half) for half in range(2)]
            low = [x_trace(ref, sigma, 0, b, half) for half in range(2)]
            for part in range(3):
                to_right = jnp.where(even_row, sub_roll(high[0][part], -1), high[1][part])
                to_left = jnp.where(even_row, low[1][part], sub_roll(low[0][part], 1))
                at = pl.ds(((number * 3 + part) * 4 + b) * 8, 8)
                first[at, :] = jnp.where(even_me, to_right, to_left)
                second[at, :] = jnp.where(even_me, to_left, to_right)
    send.wait()


def interior(ref, sigma, matrix, scale, x_low, x_high, emit):
    rows = rows_iota()
    lower = rows < 4
    m = matrix * scale

    def pair(first, second):
        return jnp.where(lower, jnp.float32(first), jnp.float32(second))

    to_low = [pair(m[0, 1], m[1, 0]), pair(m[0, 2], m[1, 3]), pair(m[0, 3], m[1, 2])]
    to_high = [pair(m[2, 0], m[3, 1]), pair(m[2, 1], m[3, 0]), pair(m[2, 3], m[3, 2])]
    lift = jnp.float32(lift_half * scale)
    six = [
        jnp.where((rows >= 2) & (rows < 4), lift, 0.0),
        jnp.where((rows >= 4) & (rows < 6), lift, 0.0),
    ]
    z_face = [lower, rows >= 4]
    lanes = lanes_iota()
    even_row = (rows & 1) == 0

    def own(count, half, inner_only):
        face = (six[half] > 0.0) if inner_only else z_face[half]
        return jnp.where(face, -lift * (count + 1), -lift * count)

    diagonal = {
        (count, half, inner): own(count, half, inner)
        for count in range(3)
        for half in range(2)
        for inner in (False, True)
    }

    def weighted(field, fixed, index, axis):
        total = None
        for other in range(4):
            if other == index:
                continue
            a, b, half = fixed
            if axis == 0:
                a = other
            else:
                b = other
            term = jnp.float32(m[index, other]) * load(ref, field, a, b, half)
            total = term if total is None else total + term
        return total

    def c_weighted(values, rolled, half):
        if half == 0:
            return to_low[0] * rolled[0] + to_low[1] * values[1] + to_low[2] * rolled[1]
        return to_high[0] * values[0] + to_high[1] * rolled[0] + to_high[2] * rolled[1]

    for a in range(4):
        for b in range(4):
            press = [load(ref, 0, a, b, h) for h in range(2)]
            vel = [[load(ref, 1 + i, a, b, h) for h in range(2)] for i in range(3)]
            press_rolled = [sub_roll(v, 4) for v in press]
            up_rolled = [sub_roll(v, 4) for v in vel[2]]
            e0, e1 = wall_traces(press, vel[2], sigma)
            z_terms = [six[0] * sub_roll(e1, -2), six[1] * sub_roll(e0, 2)]
            count = (1 if a in (0, 3) else 0) + (1 if b in (0, 3) else 0)
            for half in range(2):
                fixed = (a, b, half)
                out_p = (
                    weighted(1, fixed, a, 0)
                    + weighted(2, fixed, b, 1)
                    + c_weighted(vel[2], up_rolled, half)
                )
                out_1 = weighted(0, fixed, a, 0)
                out_2 = weighted(0, fixed, b, 1)
                out_3 = c_weighted(press, press_rolled, half)
                out_p = out_p + diagonal[count, half, False] * press[half] + z_terms[half]
                out_1 = out_1 + diagonal[count, half, True] * vel[0][half]
                out_2 = out_2 + diagonal[count, half, True] * vel[1][half]
                out_3 = out_3 + diagonal[count, half, False] * vel[2][half]
                plus = (sigma > 0) == (half == 0)
                out_3 = out_3 + z_terms[half] if plus else out_3 - z_terms[half]
                turn = -2 if half == 0 else 2
                out_1 = out_1 + six[half] * sub_roll(vel[0][1 - half], turn)
                out_2 = out_2 + six[half] * sub_roll(vel[1][1 - half], turn)
                if a in (0, 3):
                    theirs = x_trace(ref, sigma, 3 - a, b, half)
                    if a == 0:
                        near = [
                            jnp.where(even_row, x_low(part, b, half), sub_roll(t, 1))
                            for part, t in enumerate(theirs)
                        ]
                    else:
                        near = [
                            jnp.where(even_row, sub_roll(t, -1), x_high(part, b, half))
                            for part, t in enumerate(theirs)
                        ]
                    near = [lift * n for n in near]
                    out_p = out_p + near[0]
                    plus = (sigma > 0) == (a == 0)
                    out_1 = out_1 + near[0] if plus else out_1 - near[0]
                    out_2 = out_2 + near[1]
                    out_3 = out_3 + near[2]
                if b in (0, 3):
                    theirs = y_trace(ref, sigma, a, 3 - b, half)
                    if b == 0:
                        weight = jnp.where(lanes == 0, 0.0, lift)
                        near = [weight * lane_roll(t, 1) for t in theirs]
                    else:
                        weight = jnp.where(lanes == 127, 0.0, lift)
                        near = [weight * lane_roll(t, -1) for t in theirs]
                    out_p = out_p + near[0]
                    plus = (sigma > 0) == (b == 0)
                    out_2 = out_2 + near[0] if plus else out_2 - near[0]
                    out_1 = out_1 + near[1]
                    out_3 = out_3 + near[2]
                emit(a, b, half, (out_p, out_1, out_2, out_3))


def wall_traces(press, vertical, sigma):
    if sigma > 0:
        return press[0] - vertical[0], press[1] + vertical[1]
    return press[0] + vertical[0], press[1] - vertical[1]


def interior_kernel(
    st, ct, first, second, rg_in, new_st, new_rg, grad, st_out, rg_out, grad_out, rg, sems
):
    me_x = lax.axis_index("gx")
    load_rg = pltpu.make_async_copy(rg_in, rg, sems.at[3])
    load_rg.start()
    even_me = (me_x & 1) == 0

    def halos(number):
        def at(part, b):
            return pl.ds(((number * 3 + part) * 4 + b) * 8, 8)

        def x_low(part, b, half):
            got = jnp.where(even_me, second[at(part, b), :], first[at(part, b), :])
            return got if half == 0 else sub_roll(got, -1)

        def x_high(part, b, half):
            got = jnp.where(even_me, first[at(part, b), :], second[at(part, b), :])
            return got if half == 0 else sub_roll(got, 1)

        return x_low, x_high

    matrix = derivative_table()
    matrix = matrix * (1.0 - np.eye(4))

    def store(source, target, kind):
        inner = (pl.ds(1, 2), slice(None), pl.ds(16, 32))
        copy = pltpu.make_async_copy(source.at[inner], target.at[inner], sems.at[kind])
        copy.start()
        return copy

    def emit_grad(a, b, half, outs):
        at = rows_at(b, half)
        for field in range(4):
            grad[field, a, at, :] = ct[field, a, at, :] + outs[field]

    def emit_state(a, b, half, outs):
        at = rows_at(b, half)
        for field in range(4):
            following = jnp.float32(section_a) * rg[field, a, at, :] + outs[field]
            new_rg[field, a, at, :] = following
            new_st[field, a, at, :] = st[field, a, at, :] + jnp.float32(section_b) * following

    interior(ct, -1, -matrix.T, time_step * section_b, *halos(1), emit_grad)
    stores = [store(grad, grad_out, 2)]
    load_rg.wait()
    interior(st, 1, -matrix, time_step, *halos(0), emit_state)
    stores += [store(new_st, st_out, 0), store(new_rg, rg_out, 1)]
    for copy in stores:
        copy.wait()


def finish_kernel(
    gx,
    gy,
    st,
    ct,
    imp,
    wp,
    new_st,
    new_rg,
    grad,
    chunks,
    third,
    fourth,
    st_prior,
    rg_prior,
    grad_prior,
    st_out,
    rg_out,
    grad_out,
    imp_out,
    table,
    imp_grad,
    full_st,
    full_rg,
    full_grad,
    sems,
    last_sem,
):
    del st_prior, rg_prior, grad_prior
    me_y = lax.axis_index("gy")
    rows, lanes = rows_iota(), lanes_iota()
    stores = []

    def store(source, target, at, kind, piece):
        copy = pltpu.make_async_copy(source.at[at], target.at[at], sems.at[kind, piece])
        copy.start()
        stores.append(copy)

    def store_lines(source, target, b, kind):
        every = slice(None)
        if b in (0, 3):
            store(source, target, (every, every, pl.ds(b * 16, 16)), kind, b)
        if b == 2:
            for piece, field in ((1, 0), (2, 3)):
                at = (pl.ds(field, 1), every, pl.ds(16, 32))
                store(source, target, at, kind, piece)

    slots = slots_of(gx, gy)
    total = None
    per_row = gx // 4
    for y in range(gy):
        for quarter in range(4):
            parts = []
            for x in range(quarter * per_row, (quarter + 1) * per_row):
                start = slots[x * gy + y] * ROWS
                piece = chunks[start : start + 4, :]
                total = piece if total is None else total + piece
                parts.append(chunks[start + 4 : start + 5, :])
            line = functools.reduce(jnp.add, parts)
            table[y * 4 + quarter : y * 4 + quarter + 1, :] = (line - 1.0) / (line + 1.0)
    patch_sum = total
    above = imp[...] + 1.0
    factor = time_step * section_b * lift_half * 2.0
    imp_grad[...] = patch_sum * jnp.float32(factor) / (above * above)
    send_sum = pltpu.make_async_copy(imp_grad, imp_out, last_sem.at[0])
    send_sum.start()
    patch = jnp.concatenate([wp[...], wp[...]], axis=0)
    low_of = patch & (LANES - 1)
    high_of = lax.shift_right_logical(patch, 7)
    reflect = jnp.zeros((8, LANES), jnp.float32)
    for high in range(4 * gy):
        line = jnp.broadcast_to(table[high : high + 1, :], (8, LANES))
        found = jnp.take_along_axis(line, low_of, axis=1)
        reflect = jnp.where(high_of == high, found, reflect)

    even_me_y = (me_y & 1) == 0
    below = jnp.where(even_me_y, fourth[...], third[...])
    ahead = jnp.where(even_me_y, third[...], fourth[...])

    for number, ref, sigma, scale in (
        (1, ct, -1, time_step * section_b),
        (0, st, 1, time_step),
    ):
        lift = jnp.float32(lift_half * scale)
        wall = [
            jnp.where(rows < 2, reflect * lift, 0.0),
            jnp.where(rows >= 6, reflect * lift, 0.0),
        ]
        first_lane = jnp.where(lanes == 0, lift, 0.0)
        last_lane = jnp.where(lanes == LANES - 1, lift, 0.0)
        for b in (0, 3, 1, 2):
            for a in range(4):
                press = [load(ref, 0, a, b, h) for h in range(2)]
                vertical = [load(ref, 3, a, b, h) for h in range(2)]
                traces = wall_traces(press, vertical, sigma)
                for half in range(2):
                    term = wall[half] * traces[half]
                    plus = (sigma > 0) == (half == 0)
                    outs = {0: term, 3: term if plus else -term}
                    if b in (0, 3):
                        near = []
                        for part in range(3):
                            k = (number * 3 + part) * 8 + a * 2 + half
                            if b == 0:
                                near.append(first_lane * lane_roll(below, -k))
                            else:
                                near.append(last_lane * lane_roll(ahead, LANES - 1 - k))
                        outs[0] = outs[0] + near[0]
                        plus = (sigma > 0) == (b == 0)
                        outs[2] = near[0] if plus else -near[0]
                        outs[1] = near[1]
                        outs[3] = outs[3] + near[2]
                    at = rows_at(b, half)
                    for field, more in outs.items():
                        if number == 0:
                            full_rg[field, a, at, :] = new_rg[field, a, at, :] + more
                            full_st[field, a, at, :] = (
                                new_st[field, a, at, :] + jnp.float32(section_b) * more
                            )
                        else:
                            full_grad[field, a, at, :] = grad[field, a, at, :] + more
            if number == 0:
                store_lines(full_rg, rg_out, b, 1)
                store_lines(full_st, st_out, b, 0)
            else:
                store_lines(full_grad, grad_out, b, 2)
    for copy in stores:
        copy.wait()
    send_sum.wait()


def per_device(state, register, cotangent, impedance, wall_patch):
    gx, gy = lax.axis_size("gx"), lax.axis_size("gy")
    flat = (4, 4, 64, LANES)
    st, rg, ct = (v.reshape(flat) for v in (state, register, cotangent))
    imp = impedance.reshape(4, LANES)
    wp = wall_patch.reshape(4, LANES)
    f32 = jnp.float32
    any_place = pl.BlockSpec(memory_space=pltpu.HBM)
    on_chip = pl.BlockSpec(memory_space=pltpu.VMEM)
    whole = pltpu.VMEM(flat, f32)
    params = pltpu.CompilerParams(vmem_limit_bytes=8 * 2**20)
    halo = pltpu.VMEM((192, LANES), f32)
    column = pltpu.VMEM((8, LANES), f32)
    st, ct, imp, wp, first, second, third, fourth, chunks = pl.pallas_call(
        functools.partial(pack_kernel, gx, gy),
        in_specs=[any_place] * 4,
        out_specs=[on_chip] * 8 + [any_place],
        out_shape=(
            whole,
            whole,
            pltpu.VMEM((4, LANES), f32),
            pltpu.VMEM((4, LANES), jnp.int32),
            halo,
            halo,
            column,
            column,
            pltpu.HBM((gx * gy * ROWS, LANES), f32),
        ),
        scratch_shapes=[
            pltpu.VMEM((gx * gy * ROWS, LANES), f32),
            pltpu.VMEM((LANES, 4 * LANES), jnp.bfloat16),
            pltpu.SemaphoreType.DMA((2, 4)),
            pltpu.SemaphoreType.DMA((3,)),
        ],
        compiler_params=params,
        name="pack",
    )(*(pltpu.with_memory_space_constraint(v, pltpu.HBM) for v in (st, ct, imp, wp)))

    def near(count):
        return [(i, i ^ 1) for i in range(count)]

    def far(count):
        return [(i, (i + 1) % count if i % 2 else (i - 1) % count) for i in range(count)]

    first = lax.ppermute(first, "gx", near(gx))
    second = lax.ppermute(second, "gx", far(gx))
    chunks = lax.all_to_all(
        chunks.reshape(gx * gy, ROWS, 1, LANES), ("gx", "gy"), 0, 0, axis_index_groups=[group_order(gx, gy)]
    ).reshape(gx * gy * ROWS, LANES)
    third = lax.ppermute(third, "gy", near(gy))
    fourth = lax.ppermute(fourth, "gy", far(gy))
    result = pltpu.HBM(flat, f32)
    new_st, new_rg, grad, st_out, rg_out, grad_out = pl.pallas_call(
        interior_kernel,
        in_specs=[on_chip] * 4 + [any_place],
        out_specs=[on_chip] * 3 + [any_place] * 3,
        out_shape=(whole, whole, whole, result, result, result),
        scratch_shapes=[pltpu.VMEM(flat, f32), pltpu.SemaphoreType.DMA((4,))],
        compiler_params=params,
        cost_estimate=pl.CostEstimate(
            flops=INTERIOR_FLOPS, bytes_accessed=2400000, transcendentals=0
        ),
        name="interior",
    )(st, ct, first, second, pltpu.with_memory_space_constraint(rg, pltpu.HBM))
    new_st, new_rg, grad, imp_grad = pl.pallas_call(
        functools.partial(finish_kernel, gx, gy),
        in_specs=[on_chip] * 10 + [any_place] * 3,
        out_specs=[any_place] * 4,
        out_shape=(result, result, result, pltpu.HBM((4, LANES), f32)),
        input_output_aliases={10: 0, 11: 1, 12: 2},
        scratch_shapes=[
            pltpu.VMEM((4 * gy, LANES), f32),
            pltpu.VMEM((4, LANES), f32),
            pltpu.VMEM(flat, f32),
            pltpu.VMEM(flat, f32),
            pltpu.VMEM(flat, f32),
            pltpu.SemaphoreType.DMA((3, 4)),
            pltpu.SemaphoreType.DMA((1,)),
        ],
        compiler_params=params,
        name="finish",
    )(
        st,
        ct,
        imp,
        wp,
        new_st,
        new_rg,
        grad,
        chunks,
        third,
        fourth,
        st_out,
        rg_out,
        grad_out,
    )
    return (
        new_st.reshape(state.shape),
        new_rg.reshape(state.shape),
        grad.reshape(state.shape),
        imp_grad.reshape(impedance.shape),
    )


def solution(mesh):
    fields = P(None, None, None, "gx", "gy")
    return jax.shard_map(
        per_device,
        mesh=mesh,
        in_specs=(fields, fields, fields, P("gy"), P(None, "gx", "gy")),
        out_specs=(fields, fields, fields, P("gy")),
        check_vma=False,
    )
```
